32 devices in a mesh: row: 4 (over x, core), col: 8 (over z, y).
Axes of the slice: x: 2, y: 2, z: 4, core: 2. Of those that a mesh axis runs over, the one named last changes fastest.
Arguments:
- y_prev: float32 [16384, 512], P('row'), may hold values from -6 to 6
- u_cols: float32 [512, 16384], P('col', 'row'), may hold values from -0.046875 to 0.046875
- b_panel: float32 [512, 512], P('col'), may hold values from -6 to 6
- u_diag: float32 [512, 512], replicated, may hold values from -1 to 2, as said below
- l_diag: float32 [512, 512], replicated, may hold values from -1 to 1, as said below
- l_coupling: float32 [512, 512], P('col'), may hold values from -0.25 to 0.25
- l_prev_diag: float32 [512, 512], replicated, may hold values from -1 to 1, as said below
- perm: int32 [1024], P('col'), may hold values from 0 to 1023, each once
Outputs:
- y_panel: float32 [512, 512], P('col')
- x_tail: float32 [1024, 512], P('col', 'row')
The draws below stay inside these ranges and needn't reach their ends.
Inputs may be any that keep to these rules, and one draw needn't show every extreme that they name: `u_diag`: upper triangular: zero below the diagonal, diagonal between 1 and 2. `l_diag`: unit lower triangular: zero above the diagonal, ones on it. `l_prev_diag`: unit lower triangular: zero above the diagonal, ones on it.
All inputs are finite; a program needn't handle non-finite values.
Results may differ from the reference program's by a relative error of at most 0.00011.
Values sent between devices are 32-bit elements; how exact they have to be, the bound alone decides.
No kernel may reach another device: no remote copies, remote signals or barrier semaphores. Data moves between devices by JAX's collectives and lax.ppermute only.
A program may use at most 128 MiB of HBM per device.

```python
import math
import jax
import jax.numpy as jnp
from jax import lax

NB = 512
R = 512
K = 16384


def triangle(key, upper, unit):
    first, second = jax.random.split(key)
    rows = jnp.arange(NB)[:, None]
    cols = jnp.arange(NB)[None, :]
    off_part = jnp.clip(jax.random.normal(first, (NB, NB), jnp.float32), -6.0, 6.0) * (0.45 / math.sqrt(NB))
    if unit:
        diag_vals = jnp.ones((NB,), jnp.float32)
    else:
        diag_vals = jax.random.uniform(second, (NB,), jnp.float32, 1.0, 2.0)
    if upper:
        keep = cols > rows
    else:
        keep = cols < rows
    return jnp.where(rows == cols, diag_vals[None, :], jnp.where(keep, off_part, 0.0))


def draw_u_diag(key, part):
    return triangle(key, True, False)


def draw_l_diag(key, part):
    return triangle(jax.random.fold_in(key, 11), False, True)


def draw_l_prev_diag(key, part):
    return triangle(jax.random.fold_in(key, 23), False, True)


def shard_levels(key, extent, shards, smallest, top_value):
    def one(axis_at, parts):
        draws = jax.random.uniform(jax.random.fold_in(jax.random.fold_in(key, 6), axis_at), (parts,), jnp.float32, smallest / len(shards), top_value / len(shards))
        return jnp.repeat(jnp.exp(draws), extent[axis_at] // parts).reshape((-1,) + (1,) * (len(extent) - axis_at - 1))

    gain = one(*shards[0])
    for cut in shards[1:]:
        gain = gain * one(*cut)
    return gain


def scatter_about(key, extent, spread, most, pieces=(), kind=jnp.bfloat16):
    gain = shard_levels(key, extent, pieces, -0.22, 0.18) if pieces else 1.0
    drawn = jax.random.normal(key, extent, jnp.float32) * spread * gain
    return jnp.minimum(jnp.maximum(drawn, -most), most).astype(kind)


def setup_inputs(seed: int = 0) -> dict:
    key_list = jax.random.split(jax.random.key(seed), 9)
    return {
        "y_prev": scatter_about(key_list[0], (K, R), 1.0, 6.0, ((0, 4),), jnp.float32),
        "u_cols": scatter_about(key_list[1], (NB, K), K ** -0.5, 0.046875, ((0, 8), (1, 4)), jnp.float32),
        "b_panel": scatter_about(key_list[2], (NB, R), 1.0, 6.0, ((0, 8),), jnp.float32),
        "u_diag": draw_u_diag(jax.random.fold_in(key_list[8], 71), 0),
        "l_diag": draw_l_diag(jax.random.fold_in(key_list[8], 71), 0),
        "l_coupling": scatter_about(key_list[5], (NB, NB), NB ** -0.5, 0.25, ((0, 8),), jnp.float32),
        "l_prev_diag": draw_l_prev_diag(jax.random.fold_in(key_list[8], 71), 0),
        "perm": jax.random.permutation(key_list[7], 2 * NB).astype(jnp.int32),
    }


def solve_transposed(matrix, target, lower, unit):
    return lax.linalg.triangular_solve(matrix, target, left_side=True, lower=lower, transpose_a=True, unit_diagonal=unit)

def reference(y_prev, u_cols, b_panel, u_diag, l_diag, l_coupling, l_prev_diag, perm):
    high = lax.Precision.HIGHEST
    partial_value = jnp.dot(u_cols.astype(jnp.float32), y_prev.astype(jnp.float32), precision=high, preferred_element_type=jnp.float32)
    resid = b_panel - partial_value
    y_panel = solve_transposed(u_diag, resid, False, False)
    z_last = solve_transposed(l_diag, y_panel, True, True)
    couple = jnp.dot(l_coupling.T.astype(jnp.float32), z_last.astype(jnp.float32), precision=high, preferred_element_type=jnp.float32)
    y_before = y_prev[K - NB:]
    w_prev = solve_transposed(l_prev_diag, y_before - couple, True, True)
    stacked = jnp.concatenate([w_prev, z_last], axis=0)
    x_tail = jnp.take(stacked, perm, axis=0)
    return (y_panel, x_tail)
```

```python
import functools

import jax
import jax.numpy as jnp
from jax import lax
from jax.experimental import pallas as pl
from jax.experimental.pallas import tpu as pltpu
from jax.sharding import PartitionSpec as P

F32, BF16 = jnp.float32, jnp.bfloat16
TILE = 128
BASE = 16
VMEM = pl.BlockSpec(memory_space=pltpu.VMEM)
SMEM = pl.BlockSpec(memory_space=pltpu.SMEM)


def halves(value):
    high = value.astype(BF16)
    return high, (value - high.astype(F32)).astype(BF16)


def mm(left, right):
    return jnp.dot(left, right, preferred_element_type=F32)


def dot3(left, right):
    lh, ll = left if isinstance(left, tuple) else halves(left)
    rh, rl = right if isinstance(right, tuple) else halves(right)
    return mm(lh, rh) + (mm(lh, rl) + mm(ll, rh))


def tile_of(ref, i, j):
    return ref[i * TILE : (i + 1) * TILE, j * TILE : (j + 1) * TILE]


def iotas():
    shape = (TILE, TILE)
    return lax.broadcasted_iota(jnp.int32, shape, 0), lax.broadcasted_iota(jnp.int32, shape, 1)


def unit_lower_inverses(blocks):
    rows, cols = iotas()
    shift = BASE.bit_length() - 1
    same = (rows >> shift) == (cols >> shift)
    eye = (rows == cols).astype(F32)
    base = rows & ~(BASE - 1)
    found = []
    for block in blocks:
        inner = jnp.where(same & (rows > cols), block, 0.0)
        inv = eye
        for i in range(BASE - 1):
            column = jnp.take_along_axis(inner, base + i, axis=1)
            pivot = inv.reshape(TILE // BASE, BASE, TILE)[:, i : i + 1, :]
            pivot = jnp.broadcast_to(pivot, (TILE // BASE, BASE, TILE)).reshape(TILE, TILE)
            inv = inv - column * pivot
        found.append(inv)
    size = BASE
    while size < TILE:
        shift = size.bit_length() - 1
        off = ((rows >> (shift + 1)) == (cols >> (shift + 1))) & ((rows >> shift) > (cols >> shift))
        parts = [halves(inv) for inv in found]
        mids = [dot3(part, jnp.where(off, block, 0.0)) for part, block in zip(parts, blocks)]
        found = [inv - dot3(mid, part) for inv, mid, part in zip(found, mids, parts)]
        size *= 2
    return found


def prepare_kernel(u_ref, l_ref, lp_ref, perm_ref, tail_ref, use_ref, du_ref, dl_ref, a_ref, v_ref):
    width = u_ref.shape[0]
    count = width // TILE
    rows, cols = iotas()
    diag = rows == cols
    blocks, scales = [], []
    for i in range(count):
        upper = tile_of(u_ref, i, i).T
        pivot_col = 1.0 / jnp.sum(jnp.where(diag, upper, 0.0), axis=1, keepdims=True)
        pivot_row = 1.0 / jnp.sum(jnp.where(diag, upper, 0.0), axis=0, keepdims=True)
        blocks.append(upper * pivot_col)
        scales.append(pivot_row)
    blocks += [tile_of(l_ref, i, i) for i in range(count)]
    blocks += [tile_of(lp_ref, i, i) for i in range(count)]
    found = unit_lower_inverses(blocks)
    for i in range(count):
        du_ref[i * TILE : (i + 1) * TILE, :] = (found[i] * scales[i]).T
        dl_ref[i * TILE : (i + 1) * TILE, :] = found[count + i]
    inv_prev = found[2 * count :]
    perm = perm_ref[...]
    picks = perm.shape[1]
    solved = []
    for i in range(count):
        row_ids = i * TILE + lax.broadcasted_iota(jnp.int32, (TILE, picks), 0)
        remain = (row_ids == perm).astype(F32)
        for j in range(i):
            remain = remain - dot3(tile_of(lp_ref, i, j), solved[j])
        solved.append(halves(dot3(inv_prev[i], remain)))
        a_ref[i * TILE : (i + 1) * TILE, :] = solved[i][0].astype(F32) + solved[i][1].astype(F32)
    a_t = jnp.concatenate([a_ref[i * TILE : (i + 1) * TILE, :].T for i in range(count)], axis=1)
    scale = use_ref[0, 0]
    v_ref[...] = dot3(a_t, tail_ref[...]) * scale


def solve_u_kernel(resid_ref, u_ref, du_ref, where_ref, yt_ref, y_ref, full_ref):
    count = u_ref.shape[0] // TILE
    share = y_ref.shape[0]
    solved = []
    for i in range(count):
        span = slice(i * TILE, (i + 1) * TILE)
        remain = resid_ref[span, :].T
        for j in range(i):
            remain = remain - dot3(solved[j], tile_of(u_ref, j, i))
        value = dot3(remain, du_ref[span, :])
        yt_ref[:, span] = value
        full_ref[span, :] = value.T
        solved.append(halves(value))
    y_ref[...] = full_ref[pl.ds(pl.multiple_of(where_ref[0, 0] * share, share), share), :]


def finish_kernel(yt_ref, l_ref, dl_ref, lc_ref, a_ref, perm_ref, v_ref, x_ref):
    width = l_ref.shape[0]
    count = width // TILE
    perm = perm_ref[...]
    picks = perm.shape[1]
    solved = {}
    total = None
    for i in reversed(range(count)):
        span = slice(i * TILE, (i + 1) * TILE)
        remain = yt_ref[:, span]
        for j in range(i + 1, count):
            remain = remain - dot3(solved[j], tile_of(l_ref, j, i))
        solved[i] = halves(dot3(remain, dl_ref[span, :]))
        row_ids = width + i * TILE + lax.broadcasted_iota(jnp.int32, (TILE, picks), 0)
        select = (row_ids == perm).astype(F32).astype(BF16)
        term = mm(solved[i][0], select) + mm(solved[i][1], select)
        total = term if total is None else total + term
    z = tuple(jnp.concatenate([solved[i][k] for i in range(count)], axis=1) for k in range(2))
    couple = dot3(z, lc_ref[...])
    total = total - dot3(couple, a_ref[...])
    x_ref[...] = total.T + v_ref[...]


def call(kernel, outs, flops, bytes_accessed, scratch=(), **specs):
    return pl.pallas_call(
        kernel,
        out_shape=outs,
        scratch_shapes=scratch,
        cost_estimate=pl.CostEstimate(flops=flops, bytes_accessed=bytes_accessed, transcendentals=0),
        compiler_params=pltpu.CompilerParams(vmem_limit_bytes=48 << 20),
        **specs,
    )


def shape(*dims):
    return jax.ShapeDtypeStruct(dims, F32)


def inner_size(size):
    inner = 1
    while inner * inner * 4 <= size and size % (inner * 2) == 0:
        inner *= 2
    return inner


def shifted(value, axis, size, step, group):
    stride, length = group
    pairs = []
    for dst in range(size):
        place = (dst // stride) % length
        src = dst + ((place + step) % length - place) * stride
        pairs.append((src, dst))
    return lax.ppermute(value, axis, pairs)


def ordered(parts, place):
    count = len(parts)
    stack = jnp.concatenate(parts + parts[: count - 1], axis=0)
    rows = parts[0].shape[0]
    return lax.dynamic_slice_in_dim(stack, lax.rem(count - place, count) * rows, count * rows, 0)


def gather_group(value, axis, size, group):
    stride, length = group
    parts = [value] + [shifted(value, axis, size, step, group) for step in range(1, length)]
    place = lax.rem(lax.axis_index(axis) // stride, length)
    return ordered(parts, place)


def per_device(y_prev, u_cols, b_panel, u_diag, l_diag, l_coupling, l_prev_diag, perm):
    width = u_diag.shape[0]
    share = u_cols.shape[0]
    row_size, col_size = lax.axis_size("row"), lax.axis_size("col")
    row, col = lax.axis_index("row"), lax.axis_index("col")
    column_share = b_panel.shape[1] // row_size
    picks = perm.shape[0]

    coupling = lax.all_gather(l_coupling, "col", axis=0, tiled=True)
    partial_value = jnp.dot(u_cols, y_prev, precision=lax.Precision.HIGH, preferred_element_type=F32)
    perm_row = jnp.pad(perm, (0, max(TILE - picks, 0)), constant_values=-1)[None, :]
    lanes = perm_row.shape[1]
    use = (row == row_size - 1).astype(F32).reshape(1, 1)
    tail = y_prev[y_prev.shape[0] - width :]
    du, dl, a, v = call(
        prepare_kernel,
        (shape(width, TILE), shape(width, TILE), shape(width, lanes), shape(lanes, b_panel.shape[1])),
        1 << 30,
        6 << 20,
        in_specs=[VMEM] * 5 + [SMEM],
        out_specs=[VMEM] * 4,
    )(u_diag, l_diag, l_prev_diag, perm_row, tail, use)

    payload = jnp.concatenate([partial_value, v], axis=0)
    blocks = lambda place: lax.dynamic_slice_in_dim(payload, place * column_share, column_share, 1)
    own = blocks(row)
    for step in range(1, row_size):
        target = lax.rem(row + row_size - step, row_size)
        own = own + shifted(blocks(target), "row", row_size, step, (1, row_size))
    mine = lax.dynamic_slice_in_dim(b_panel, row * column_share, column_share, 1)
    resid = mine - own[:share]
    v_mine = own[share:]

    inner = inner_size(col_size)
    resid = gather_group(resid, "col", col_size, (1, inner))
    resid = gather_group(resid, "col", col_size, (inner, col_size // inner))

    rhs = max(TILE, column_share)
    widen = lambda value: jnp.pad(value, ((0, 0), (0, rhs - value.shape[1])))
    where = col.astype(jnp.int32).reshape(1, 1)
    yt, y_mine = call(
        solve_u_kernel,
        (shape(rhs, width), shape(share, rhs)),
        200 << 20,
        2 << 20,
        scratch=[pltpu.VMEM((width, rhs), F32)],
        in_specs=[VMEM] * 3 + [SMEM],
        out_specs=[VMEM] * 2,
    )(widen(resid), u_diag, du, where)
    y_part = lax.all_gather(y_mine[:, :column_share], "row", axis=1, tiled=True)

    x = call(
        finish_kernel,
        shape(lanes, rhs),
        400 << 20,
        4 << 20,
        in_specs=[VMEM] * 7,
        out_specs=VMEM,
    )(yt, l_diag, dl, coupling, a, perm_row, widen(v_mine))
    return (y_part, x[:picks, :column_share])


def solution(mesh):
    return jax.shard_map(
        per_device,
        mesh=mesh,
        in_specs=(
            P("row", None),
            P("col", "row"),
            P("col", None),
            P(),
            P(),
            P("col", None),
            P(),
            P("col"),
        ),
        out_specs=(P("col", None), P("col", "row")),
        check_vma=False,
    )
```

```python
import functools

import jax
import jax.numpy as jnp
from jax import lax
from jax.experimental import pallas as pl
from jax.experimental.pallas import tpu as pltpu
from jax.sharding import PartitionSpec as P

F32, BF16 = jnp.float32, jnp.bfloat16
TILE = 128
VMEM = pl.BlockSpec(memory_space=pltpu.VMEM)
SMEM = pl.BlockSpec(memory_space=pltpu.SMEM)
HBM = pl.BlockSpec(memory_space=pltpu.HBM)


def halves(value):
    high = value.astype(BF16)
    return high, (value - high.astype(F32)).astype(BF16)


def mm(left, right):
    return jnp.dot(left, right, preferred_element_type=F32)


def dot3(left, right):
    lh, ll = left if isinstance(left, tuple) else halves(left)
    rh, rl = right if isinstance(right, tuple) else halves(right)
    return mm(lh, rh) + (mm(lh, rl) + mm(ll, rh))


def joined(left, right):
    lh, ll = left
    rh, rl = right
    across = jnp.concatenate([jnp.concatenate([rh, rh], axis=0), jnp.concatenate([rl, jnp.zeros_like(rl)], axis=0)], axis=1)
    both = mm(jnp.concatenate([lh, ll], axis=1), across)
    return both[:, : rh.shape[1]] + both[:, rh.shape[1] :]


def tile_of(ref, i, j):
    return ref[i * TILE : (i + 1) * TILE, j * TILE : (j + 1) * TILE]


def iotas():
    shape = (TILE, TILE)
    return lax.broadcasted_iota(jnp.int32, shape, 0), lax.broadcasted_iota(jnp.int32, shape, 1)


def unit_lower_inverses(blocks):
    rows, cols = iotas()
    eye = (rows == cols).astype(F32)
    first = ((rows >> 1) == (cols >> 1)) & (rows > cols)
    found = [eye - jnp.where(first, block, 0.0) for block in blocks]
    pieces = [halves(block) for block in blocks]
    none = jnp.zeros((TILE, TILE), BF16)
    for shift in range(1, TILE.bit_length() - 1):
        off = ((rows >> (shift + 1)) == (cols >> (shift + 1))) & ((rows >> shift) > (cols >> shift))
        parts = [halves(inv) for inv in found]
        mids = [
            halves(joined(part, tuple(jnp.where(off, half, none) for half in piece)))
            for part, piece in zip(parts, pieces)
        ]
        found = [inv - joined(mid, part) for inv, mid, part in zip(found, mids, parts)]
    return found


def product_kernel(chunk, u_cols_ref, y_ref, out_ref, y_buf, u_buf, sems):
    steps = y_buf.shape[0]
    share = out_ref.shape[0]
    copies = []
    for k in range(steps):
        span = pl.ds(k * chunk, chunk)
        copies.append(
            (
                pltpu.make_async_copy(u_cols_ref.at[:, span], u_buf.at[k], sems.at[0, k]),
                pltpu.make_async_copy(y_ref.at[span, :], y_buf.at[k], sems.at[1, k]),
            )
        )
    for pair in copies:
        for copy in pair:
            copy.start()
    total = jnp.zeros(out_ref.shape, F32)
    for k in range(steps):
        for copy in copies[k]:
            copy.wait()
        lh, ll = halves(u_buf[k])
        rh, rl = halves(y_buf[k])
        top = mm(jnp.concatenate([lh, ll], axis=0), rh)
        total = total - (top[:share] + top[share:] + mm(lh, rl))
    out_ref[...] = total


def prepare_kernel(sends, row_ref, part_ref, perm_ref, after_ref, b_hbm, u_hbm, l_hbm, lp_hbm, y_hbm, *refs):
    du_ref, dl_ref, a_ref = refs[:3]
    out_refs = refs[3:-7]
    b_ref, u_ref, l_ref, lp_ref, tail_ref, sems, pay_ref = refs[-7:]
    width = u_ref.shape[0]
    rest = y_hbm.shape[0] - width
    sources = [
        (u_hbm, u_ref),
        (l_hbm, l_ref),
        (lp_hbm, lp_ref),
        (y_hbm.at[pl.ds(rest, width), :], tail_ref),
        (b_hbm, b_ref),
    ]
    copies = [pltpu.make_async_copy(src, dst, sems.at[k]) for k, (src, dst) in enumerate(sources)]
    for copy in copies:
        copy.start()
    share = part_ref.shape[0]
    count = width // TILE
    rows, cols = iotas()
    diag = rows == cols
    blocks, scales = [], []
    copies[0].wait()
    for i in range(count):
        upper = tile_of(u_ref, i, i).T
        only = jnp.where(diag, upper, 0.0)
        blocks.append(upper * (1.0 / jnp.sum(only, axis=1, keepdims=True)))
        scales.append(1.0 / jnp.sum(only, axis=0, keepdims=True))
    copies[1].wait()
    blocks += [tile_of(l_ref, i, i) for i in range(count)]
    copies[2].wait()
    blocks += [tile_of(lp_ref, i, i) for i in range(count)]
    found = unit_lower_inverses(blocks)
    for i in range(count):
        du_ref[i * TILE : (i + 1) * TILE, :] = (found[i] * scales[i]).T
        dl_ref[i * TILE : (i + 1) * TILE, :] = found[count + i]
    perm = perm_ref[...]
    picks = perm.shape[1]
    solved, turned = [], []
    for i in range(count):
        row_ids = i * TILE + lax.broadcasted_iota(jnp.int32, (TILE, picks), 0)
        remain = (row_ids == perm).astype(F32)
        for j in range(i):
            remain = remain - joined(halves(tile_of(lp_ref, i, j)), solved[j])
        value = joined(halves(found[2 * count + i]), halves(remain))
        solved.append(halves(value))
        turned.append(value.T)
        a_ref[i * TILE : (i + 1) * TILE, :] = value
    copies[3].wait()
    copies[4].wait()
    row = row_ref[0, 0]
    size = sends + 1
    use = (row == size - 1).astype(F32)
    pay_ref[:share, :] = part_ref[...]
    pay_ref[share:, :] = dot3(jnp.concatenate(turned, axis=1), tail_ref[...]) * use
    if len(out_refs) == 1:
        out_refs[0][...] = pay_ref[...]
        return
    column_share = width // size
    for step, out_ref in enumerate(out_refs):
        target = lax.rem(row + size - step, size)
        columns = pl.ds(pl.multiple_of(target * column_share, column_share), column_share)
        out_ref[...] = pay_ref[:, columns]
        if step == 0:
            out_ref[:share, :] = out_ref[:share, :] + b_ref[:, columns]


def place_piece(col, inner, outer, share, step, piece, full_ref, columns):
    low, high = lax.rem(col, inner), lax.div(col, inner)
    high_at = lax.rem(high + step, outer)
    for turn in range(inner):
        at = high_at * inner + lax.rem(low + turn, inner)
        start = pl.multiple_of(at * share, share)
        full_ref[pl.ds(start, share), columns] = piece[turn * share : (turn + 1) * share, :]


def solve_u_kernel(inner, outer, share, col_ref, u_ref, du_ref, *refs):
    piece_refs = refs[:outer]
    yt_ref, y_ref, full_ref = refs[outer:]
    col = col_ref[0, 0]
    for step, piece_ref in enumerate(piece_refs):
        place_piece(col, inner, outer, share, step, piece_ref[...], full_ref, slice(None))
    count = u_ref.shape[0] // TILE
    solved = []
    for i in range(count):
        span = slice(i * TILE, (i + 1) * TILE)
        remain = full_ref[span, :].T
        for j in range(i):
            remain = remain - joined(solved[j], halves(tile_of(u_ref, j, i)))
        value = joined(halves(remain), halves(du_ref[span, :]))
        yt_ref[:, span] = value
        full_ref[span, :] = value.T
        solved.append(halves(value))
    y_ref[...] = full_ref[pl.ds(pl.multiple_of(col * share, share), share), :]


def finish_kernel(inner, outer, share, sides, col_ref, row_ref, yt_ref, l_ref, dl_ref, a_ref, perm_ref, v_ref, *refs):
    side_refs = refs[:sides]
    x_ref, lc_ref = refs[sides:]
    rows = inner * share
    for step, side_ref in enumerate(side_refs):
        half = side_ref.shape[1]
        at = lax.rem(row_ref[0, 0] + step, sides)
        columns = pl.ds(pl.multiple_of(at * half, half), half)
        for piece in range(outer):
            place_piece(col_ref[0, 0], inner, outer, share, piece, side_ref[piece * rows : (piece + 1) * rows, :], lc_ref, columns)
    width = l_ref.shape[0]
    count = width // TILE
    perm = perm_ref[...]
    picks = perm.shape[1]
    solved = {}
    total = None
    for i in reversed(range(count)):
        span = slice(i * TILE, (i + 1) * TILE)
        remain = yt_ref[:, span]
        for j in range(i + 1, count):
            remain = remain - joined(solved[j], halves(tile_of(l_ref, j, i)))
        solved[i] = halves(joined(halves(remain), halves(dl_ref[span, :])))
        row_ids = width + i * TILE + lax.broadcasted_iota(jnp.int32, (TILE, picks), 0)
        select = (row_ids == perm).astype(F32).astype(BF16)
        term = mm(solved[i][0], select) + mm(solved[i][1], select)
        total = term if total is None else total + term
    z = tuple(jnp.concatenate([solved[i][k] for i in range(count)], axis=1) for k in range(2))
    couple = dot3(z, lc_ref[...])
    total = total - dot3(couple, a_ref[...])
    x_ref[...] = total.T + v_ref[...]


def merge_kernel(row_ref, *refs):
    out_ref = refs[-1]
    size = len(refs) - 1
    for step, ref in enumerate(refs[:-1]):
        at = lax.rem(row_ref[0, 0] + step, size)
        columns = ref.shape[1]
        out_ref[:, pl.ds(pl.multiple_of(at * columns, columns), columns)] = ref[...]


def call(kernel, outs, flops, bytes_accessed, limit, scratch=(), **specs):
    return pl.pallas_call(
        kernel,
        out_shape=outs,
        scratch_shapes=scratch,
        cost_estimate=pl.CostEstimate(flops=flops, bytes_accessed=bytes_accessed, transcendentals=0),
        compiler_params=pltpu.CompilerParams(vmem_limit_bytes=limit << 20),
        **specs,
    )


def shape(*dims):
    return jax.ShapeDtypeStruct(dims, F32)


def in_hbm(array):
    return pltpu.with_memory_space_constraint(array, pltpu.HBM)


def inner_size(size):
    inner = 1
    while inner * inner * 4 <= size and size % (inner * 2) == 0:
        inner *= 2
    return inner


def shifted(value, axis, size, step, stride, length):
    pairs = []
    for dst in range(size):
        place = (dst // stride) % length
        pairs.append((dst + ((place + step) % length - place) * stride, dst))
    return lax.ppermute(value, axis, pairs)


def gather_pieces(value, axis, size, inner):
    near = [value] + [shifted(value, axis, size, step, 1, inner) for step in range(1, inner)]
    near = jnp.concatenate(near, axis=0)
    outer = size // inner
    return [near] + [shifted(near, axis, size, step, inner, outer) for step in range(1, outer)]


def per_device(y_prev, u_cols, b_panel, u_diag, l_diag, l_coupling, l_prev_diag, perm):
    width = u_diag.shape[0]
    share = u_cols.shape[0]
    row_size, col_size = lax.axis_size("row"), lax.axis_size("col")
    row, col = lax.axis_index("row"), lax.axis_index("col")
    columns = b_panel.shape[1]
    column_share = columns // row_size
    picks = perm.shape[0]
    aligned = column_share % TILE == 0
    row_at = row.astype(jnp.int32).reshape(1, 1)
    col_at = col.astype(jnp.int32).reshape(1, 1)
    inner = inner_size(col_size)
    outer = col_size // inner

    sides = 2 if row_size % 2 == 0 and width % (2 * TILE) == 0 else 1
    side = lax.rem(row, sides)
    half = width // sides
    coupling = gather_pieces(
        lax.dynamic_slice_in_dim(l_coupling, side * half, half, 1), "col", col_size, inner
    )

    perm_row = jnp.pad(perm, (0, max(TILE - picks, 0)), constant_values=-1)[None, :]
    lanes = perm_row.shape[1]
    steps = y_prev.shape[0] // width
    sent = share + lanes
    outs = [shape(sent, column_share)] * row_size if aligned else [shape(sent, columns)]
    part = call(
        functools.partial(product_kernel, width),
        shape(share, columns),
        1 << 30,
        9 << 20,
        24,
        scratch=[
            pltpu.VMEM((steps, width, columns), F32),
            pltpu.VMEM((steps, share, width), F32),
            pltpu.SemaphoreType.DMA((2, steps)),
        ],
        in_specs=[HBM] * 2,
        out_specs=VMEM,
    )(in_hbm(u_cols), in_hbm(y_prev))
    du, dl, a, *payload = call(
        functools.partial(prepare_kernel, row_size - 1),
        [shape(width, TILE), shape(width, TILE), shape(width, lanes)] + outs,
        1 << 30,
        5 << 20,
        12,
        scratch=[
            pltpu.VMEM(b_panel.shape, F32),
            pltpu.VMEM((width, width), F32),
            pltpu.VMEM((width, width), F32),
            pltpu.VMEM((width, width), F32),
            pltpu.VMEM((width, columns), F32),
            pltpu.SemaphoreType.DMA((5,)),
            pltpu.VMEM((sent, columns), F32),
        ],
        in_specs=[SMEM, VMEM, VMEM, pl.BlockSpec(memory_space=pl.ANY)] + [HBM] * 5,
        out_specs=[VMEM] * (3 + len(outs)),
    )(row_at, part, perm_row, coupling[0], *map(in_hbm, (b_panel, u_diag, l_diag, l_prev_diag, y_prev)))

    if aligned:
        own = payload[0]
        others = payload[1:]
    else:
        block = lambda array, place: lax.dynamic_slice_in_dim(array, place * column_share, column_share, 1)
        own = block(payload[0], row) + jnp.pad(block(b_panel, row), ((0, lanes), (0, 0)))
        others = [block(payload[0], lax.rem(row + row_size - step, row_size)) for step in range(1, row_size)]
    for step, other in enumerate(others):
        own = own + shifted(other, "row", row_size, step + 1, 1, row_size)
    rhs = max(TILE, column_share)
    widen = lambda value: jnp.pad(value, ((0, 0), (0, rhs - value.shape[1])))
    own, coupling = lax.optimization_barrier((own, coupling))
    if sides == 2:
        coupling = jnp.concatenate(coupling, axis=0)
        coupling = [coupling, shifted(coupling, "row", row_size, 1, 1, 2)]
    else:
        coupling = [jnp.concatenate(coupling, axis=0)]
    pieces = gather_pieces(widen(own[:share]), "col", col_size, inner)

    yt, y_mine = call(
        functools.partial(solve_u_kernel, inner, outer, share),
        (shape(rhs, width), shape(share, rhs)),
        200 << 20,
        2 << 20,
        8,
        scratch=[pltpu.VMEM((width, rhs), F32)],
        in_specs=[SMEM] + [VMEM] * (2 + outer),
        out_specs=[VMEM] * 2,
    )(col_at, u_diag, du, *pieces)

    if aligned:
        blocks = [y_mine] + [shifted(y_mine, "row", row_size, step, 1, row_size) for step in range(1, row_size)]
        y_part = call(merge_kernel, shape(share, columns), 0, 1 << 17, 4, in_specs=[SMEM] + [VMEM] * row_size, out_specs=VMEM)(
            row_at, *blocks
        )
    else:
        y_part = lax.all_gather(y_mine[:, :column_share], "row", axis=1, tiled=True)

    x = call(
        functools.partial(finish_kernel, inner, outer, share, sides),
        shape(lanes, rhs),
        400 << 20,
        4 << 20,
        8,
        scratch=[pltpu.VMEM((width, width), F32)],
        in_specs=[SMEM] * 2 + [VMEM] * (6 + sides),
        out_specs=VMEM,
    )(col_at, row_at, yt, l_diag, dl, a, perm_row, widen(own[share:]), *coupling)
    return (y_part, x[:picks, :column_share])


def solution(mesh):
    return jax.shard_map(
        per_device,
        mesh=mesh,
        in_specs=(
            P("row", None),
            P("col", "row"),
            P("col", None),
            P(),
            P(),
            P("col", None),
            P(),
            P("col"),
        ),
        out_specs=(P("col", None), P("col", "row")),
        check_vma=False,
    )
```

```python
import functools

import jax
import jax.numpy as jnp
from jax import lax
from jax.experimental import pallas as pl
from jax.experimental.pallas import tpu as pltpu
from jax.sharding import PartitionSpec as P

F32, BF16 = jnp.float32, jnp.bfloat16
TILE = 128
VMEM = pl.BlockSpec(memory_space=pltpu.VMEM)
SMEM = pl.BlockSpec(memory_space=pltpu.SMEM)
HBM = pl.BlockSpec(memory_space=pltpu.HBM)
ANY = pl.BlockSpec(memory_space=pl.ANY)


def halves(value):
    high = value.astype(BF16)
    return high, (value - high.astype(F32)).astype(BF16)


def mm(left, right):
    return jnp.dot(left, right, preferred_element_type=F32)


def mm_t(left, right):
    return lax.dot_general(left, right, (((1,), (1,)), ((), ())), preferred_element_type=F32)


def dot3(left, right):
    lh, ll = left if isinstance(left, tuple) else halves(left)
    rh, rl = right if isinstance(right, tuple) else halves(right)
    return mm(lh, rh) + (mm(lh, rl) + mm(ll, rh))


def joined(left, right):
    lh, ll = left
    rh, rl = right
    across = jnp.concatenate([jnp.concatenate([rh, rh], axis=0), jnp.concatenate([rl, jnp.zeros_like(rl)], axis=0)], axis=1)
    both = mm(jnp.concatenate([lh, ll], axis=1), across)
    return both[:, : rh.shape[1]] + both[:, rh.shape[1] :]


def tile_of(ref, i, j):
    return ref[i * TILE : (i + 1) * TILE, j * TILE : (j + 1) * TILE]


def iotas():
    shape = (TILE, TILE)
    return lax.broadcasted_iota(jnp.int32, shape, 0), lax.broadcasted_iota(jnp.int32, shape, 1)


def unit_lower_inverses(blocks):
    rows, cols = iotas()
    eye = (rows == cols).astype(F32)
    first = ((rows >> 1) == (cols >> 1)) & (rows > cols)
    found = [eye - jnp.where(first, block, 0.0) for block in blocks]
    pieces = [halves(block) for block in blocks]
    none = jnp.zeros((TILE, TILE), BF16)
    for shift in range(1, TILE.bit_length() - 1):
        off = ((rows >> (shift + 1)) == (cols >> (shift + 1))) & ((rows >> shift) > (cols >> shift))
        parts = [halves(inv) for inv in found]
        mids = [
            halves(joined(part, tuple(jnp.where(off, half, none) for half in piece)))
            for part, piece in zip(parts, pieces)
        ]
        found = [inv - joined(mid, part) for inv, mid, part in zip(found, mids, parts)]
    return found


def started(copies):
    for copy in copies:
        copy.start()
    return copies


def invert_kernel(
    perm_hbm, u_hbm, l_hbm, lp_hbm, du_hbm, dl_hbm, at_ref, perm_ref, u_ref, l_ref, lp_ref, du_ref, dl_ref, sems
):
    width = lp_ref.shape[0]
    count = width // TILE
    spans = [slice(i * TILE, (i + 1) * TILE) for i in range(count)]
    tiles = [pl.ds(i * TILE, TILE) for i in range(count)]
    copies = started(
        [
            pltpu.make_async_copy(src.at[tiles[i], tiles[i]], dst.at[tiles[i], :], sems.at[k, i])
            for k, (src, dst) in enumerate([(u_hbm, u_ref), (l_hbm, l_ref)])
            for i in range(count)
        ]
        + [pltpu.make_async_copy(lp_hbm, lp_ref, sems.at[2, 0]), pltpu.make_async_copy(perm_hbm, perm_ref, sems.at[3, 0])]
    )
    for copy in copies:
        copy.wait()
    rows, cols = iotas()
    diag = rows == cols
    blocks, scales = [], []
    for span in spans:
        upper = u_ref[span, :].T
        only = jnp.where(diag, upper, 0.0)
        blocks.append(upper * (1.0 / jnp.sum(only, axis=1, keepdims=True)))
        scales.append(1.0 / jnp.sum(only, axis=0, keepdims=True))
    blocks += [l_ref[span, :] for span in spans]
    blocks += [tile_of(lp_ref, i, i) for i in range(count)]
    found = unit_lower_inverses(blocks)
    for i, span in enumerate(spans):
        du_ref[span, :] = (found[i] * scales[i]).T
        dl_ref[span, :] = found[count + i]
    out = started(
        [pltpu.make_async_copy(du_ref, du_hbm, sems.at[4, 0]), pltpu.make_async_copy(dl_ref, dl_hbm, sems.at[5, 0])]
    )
    perm = perm_ref[...]
    picks = perm.shape[1]
    solved = []
    for i, span in enumerate(spans):
        row_ids = i * TILE + lax.broadcasted_iota(jnp.int32, (TILE, picks), 0)
        remain = (row_ids == perm).astype(F32)
        for j in range(i):
            remain = remain - joined(halves(tile_of(lp_ref, i, j)), solved[j])
        value = joined(halves(found[2 * count + i]), halves(remain))
        solved.append(halves(value))
        at_ref[:, span] = value.T
    for copy in out:
        copy.wait()


def product_kernel(size, paired, row_ref, at_ref, after_ref, b_ref, u_cols_ref, y_ref, *refs):
    del after_ref
    out_refs, pay_ref = refs[:-1], refs[-1]
    share = b_ref.shape[0]
    chunk = at_ref.shape[1]
    steps = y_ref.shape[0] // chunk
    total = jnp.zeros(b_ref.shape, F32)
    for k in range(steps):
        lh, ll = halves(u_cols_ref[:, k * chunk : (k + 1) * chunk])
        rh, rl = halves(y_ref[k * chunk : (k + 1) * chunk, :])
        if k == steps - 1:
            ah, al = halves(at_ref[...])
            seen = mm(ah, rh) + (mm(ah, rl) + mm(al, rh))
        top = mm(jnp.concatenate([lh, ll], axis=0), rh)
        total = total - (top[:share] + top[share:] + mm(lh, rl))
    row = row_ref[0, 0]
    pay_ref[:share, :] = total
    pay_ref[share:, :] = seen * (row == size - 1).astype(F32)
    if not paired:
        out_refs[0][...] = pay_ref[...]
        return
    columns = b_ref.shape[1] // size
    chips = size // 2
    chip, core = lax.div(row, 2), lax.rem(row, 2)
    for out_ref, side in zip(out_refs, (core, 1 - core)):
        for step in range(chips):
            place = 2 * (chip ^ step) + side
            out_ref[:, step * columns : (step + 1) * columns] = pay_ref[:, aligned_span(place, columns)]
    keep_ref = out_refs[0]
    keep_ref[:share, :columns] = keep_ref[:share, :columns] + b_ref[:, aligned_span(row, columns)]


def aligned_span(place, size):
    return pl.ds(pl.multiple_of(place * size, size), size)


def place_piece(col, inner, outer, share, step, piece, full_ref, columns):
    low, high = lax.rem(col, inner), lax.div(col, inner)
    for turn in range(outer):
        at = (high ^ turn) * inner + (low ^ step)
        full_ref[aligned_span(at, share), columns] = piece[turn * share : (turn + 1) * share, :]


def solve_u_kernel(inner, outer, share, col_ref, u_ref, du_any, *refs):
    piece_refs = refs[:inner]
    yt_ref, y_ref, full_ref, du_ref, sem = refs[inner:]
    copy = pltpu.make_async_copy(du_any, du_ref, sem)
    copy.start()
    col = col_ref[0, 0]
    for step, piece_ref in enumerate(piece_refs):
        place_piece(col, inner, outer, share, step, piece_ref[...], full_ref, slice(None))
    copy.wait()
    count = u_ref.shape[0] // TILE
    solved = []
    for i in range(count):
        span = slice(i * TILE, (i + 1) * TILE)
        remain = full_ref[span, :].T
        for j in range(i):
            remain = remain - joined(solved[j], halves(tile_of(u_ref, j, i)))
        value = joined(halves(remain), halves(du_ref[span, :]))
        yt_ref[:, span] = value
        full_ref[span, :] = value.T
        solved.append(halves(value))
    y_ref[...] = full_ref[aligned_span(col, share), :]


def finish_kernel(inner, outer, share, parts, col_ref, row_ref, yt_ref, l_ref, dl_any, at_any, perm_ref, v_any, *refs):
    side_refs = refs[: 1 if parts == 1 else 2]
    x_ref, lc_ref, dl_ref, at_ref, v_ref, sems = refs[len(side_refs) :]
    copies = started(
        [
            pltpu.make_async_copy(src, dst, sems.at[k])
            for k, (src, dst) in enumerate([(dl_any, dl_ref), (at_any, at_ref), (v_any, v_ref)])
        ]
    )
    row, col = row_ref[0, 0], col_ref[0, 0]
    rows = outer * share
    columns = lc_ref.shape[1] // parts
    chips = max(parts // 2, 1)
    for turn, side_ref in enumerate(side_refs):
        for step in range(chips):
            if parts == 1:
                target = slice(None)
            else:
                target = aligned_span(row ^ (2 * step) ^ turn, columns)
            for piece in range(inner):
                value = side_ref[piece * rows : (piece + 1) * rows, step * columns : (step + 1) * columns]
                place_piece(col, inner, outer, share, piece, value, lc_ref, target)
    for copy in copies:
        copy.wait()
    width = l_ref.shape[0]
    count = width // TILE
    perm = perm_ref[...]
    picks = perm.shape[1]
    solved = {}
    total = None
    for i in reversed(range(count)):
        span = slice(i * TILE, (i + 1) * TILE)
        remain = yt_ref[:, span]
        for j in range(i + 1, count):
            remain = remain - joined(solved[j], halves(tile_of(l_ref, j, i)))
        solved[i] = halves(joined(halves(remain), halves(dl_ref[span, :])))
        row_ids = width + i * TILE + lax.broadcasted_iota(jnp.int32, (TILE, picks), 0)
        select = (row_ids == perm).astype(F32).astype(BF16)
        term = mm(solved[i][0], select) + mm(solved[i][1], select)
        total = term if total is None else total + term
    z = tuple(jnp.concatenate([solved[i][k] for i in range(count)], axis=1) for k in range(2))
    couple = dot3(z, lc_ref[...])
    ch, cl = halves(couple)
    ah, al = halves(at_ref[...])
    total = total - (mm_t(ch, ah) + (mm_t(ch, al) + mm_t(cl, ah)))
    x_ref[...] = total.T + v_ref[...]


def merge_kernel(row_ref, after_ref, *refs):
    del after_ref
    out_ref = refs[-1]
    for step, ref in enumerate(refs[:-1]):
        out_ref[:, aligned_span(row_ref[0, 0] ^ step, ref.shape[1])] = ref[...]


def call(kernel, outs, flops, bytes_accessed, limit, scratch=(), **specs):
    return pl.pallas_call(
        kernel,
        out_shape=outs,
        scratch_shapes=scratch,
        cost_estimate=pl.CostEstimate(flops=flops, bytes_accessed=bytes_accessed, transcendentals=0),
        compiler_params=pltpu.CompilerParams(vmem_limit_bytes=limit << 20),
        **specs,
    )


def shape(*dims):
    return jax.ShapeDtypeStruct(dims, F32)


def in_hbm(array):
    return pltpu.with_memory_space_constraint(array, pltpu.HBM)


def inner_size(size):
    inner = 1
    while inner * inner * 4 <= size and size % (inner * 2) == 0:
        inner *= 2
    return inner


def swapped(value, axis, size, mask):
    return lax.ppermute(value, axis, [(dst ^ mask, dst) for dst in range(size)])


def gather_line(value, axis, size, inner):
    return jnp.concatenate([value] + [swapped(value, axis, size, mask) for mask in range(inner, size, inner)], axis=0)


def gather_pieces(line, axis, size, inner):
    return [line] + [swapped(line, axis, size, mask) for mask in range(1, inner)]


def per_device(y_prev, u_cols, b_panel, u_diag, l_diag, l_coupling, l_prev_diag, perm):
    width = u_diag.shape[0]
    share = u_cols.shape[0]
    row_size, col_size = lax.axis_size("row"), lax.axis_size("col")
    assert row_size & (row_size - 1) == 0 and col_size & (col_size - 1) == 0
    row, col = lax.axis_index("row"), lax.axis_index("col")
    columns = b_panel.shape[1]
    column_share = columns // row_size
    picks = perm.shape[0]
    paired = row_size % 2 == 0 and column_share % TILE == 0
    chips = row_size // 2
    row_at = row.astype(jnp.int32).reshape(1, 1)
    col_at = col.astype(jnp.int32).reshape(1, 1)
    inner = inner_size(col_size)
    outer = col_size // inner

    parts = row_size if paired and width % (row_size * TILE) == 0 else 1
    quarter = width // parts
    line = lax.dynamic_slice_in_dim(l_coupling, lax.rem(row, parts) * quarter, quarter, 1)
    lines = []
    mask = inner
    while mask < col_size:
        line = jnp.concatenate([line, swapped(line, "col", col_size, mask)], axis=0)
        lines.append(line)
        mask *= 2

    perm_row = jnp.pad(perm, (0, max(TILE - picks, 0)), constant_values=-1)[None, :]
    lanes = perm_row.shape[1]
    sent = share + lanes
    du, dl, at = call(
        invert_kernel,
        [shape(width, TILE), shape(width, TILE), shape(lanes, width)],
        6 << 30,
        2 << 20,
        10,
        scratch=[
            pltpu.VMEM(perm_row.shape, jnp.int32),
            pltpu.VMEM((width, TILE), F32),
            pltpu.VMEM((width, TILE), F32),
            pltpu.VMEM((width, width), F32),
            pltpu.VMEM((width, TILE), F32),
            pltpu.VMEM((width, TILE), F32),
            pltpu.SemaphoreType.DMA((6, width // TILE)),
        ],
        in_specs=[HBM] * 4,
        out_specs=[HBM, HBM, VMEM],
    )(*map(in_hbm, (perm_row, u_diag, l_diag, l_prev_diag)))
    outs = [shape(sent, columns // 2)] * 2 if paired else [shape(sent, columns)]
    payload = call(
        functools.partial(product_kernel, row_size, paired),
        outs,
        1 << 30,
        10 << 20,
        12,
        scratch=[pltpu.VMEM((sent, columns), F32)],
        in_specs=[SMEM, VMEM, ANY] + [VMEM] * 3,
        out_specs=[VMEM] * len(outs),
    )(row_at, at, lines[0], b_panel, u_cols, y_prev)

    payload, line = lax.optimization_barrier((payload, line))
    far = gather_pieces(line, "col", col_size, inner)
    mine = jnp.concatenate(far, axis=0)
    if paired:
        keep = payload[0] + swapped(payload[1], "row", row_size, 1)
        turn = lambda step: slice(step * column_share, (step + 1) * column_share)
        resid = keep[:share, turn(0)]
        for step in range(1, chips):
            resid = resid + swapped(keep[:share, turn(step)], "row", row_size, 2 * step)
        v = keep[share:, turn(0)]
    else:
        block = lambda array, place: lax.dynamic_slice_in_dim(array, place * column_share, column_share, 1)
        own = block(payload[0], row)
        for step in range(1, row_size):
            own = own + swapped(block(payload[0], row ^ step), "row", row_size, step)
        resid = own[:share] + block(b_panel, row)
        v = own[share:]
    rhs = max(TILE, column_share)
    resid, mine = lax.optimization_barrier((resid, mine))
    resid = jnp.pad(resid, ((0, 0), (0, rhs - column_share)))
    sides = [mine]
    for step in range(1, chips if paired else 1):
        if parts > 1:
            got = swapped(jnp.concatenate([mine, keep[share:, turn(step)]], axis=0), "row", row_size, 2 * step)
            sides.append(got[:width])
            v = v + got[width:]
        else:
            v = v + swapped(keep[share:, turn(step)], "row", row_size, 2 * step)
    v = jnp.pad(v, ((0, 0), (0, rhs - column_share)))
    pieces = gather_pieces(gather_line(resid, "col", col_size, inner), "col", col_size, inner)

    yt, y_mine = call(
        functools.partial(solve_u_kernel, inner, outer, share),
        (shape(rhs, width), shape(share, rhs)),
        200 << 20,
        2 << 20,
        8,
        scratch=[pltpu.VMEM((width, rhs), F32), pltpu.VMEM((width, TILE), F32), pltpu.SemaphoreType.DMA],
        in_specs=[SMEM, VMEM, ANY] + [VMEM] * inner,
        out_specs=[VMEM] * 2,
    )(col_at, u_diag, du, *pieces)

    yt, sides = lax.optimization_barrier((yt, sides))
    mine = jnp.concatenate(sides, axis=1)
    coupling = [mine, swapped(mine, "row", row_size, 1)] if parts > 1 else [mine]
    x = call(
        functools.partial(finish_kernel, inner, outer, share, parts),
        shape(lanes, rhs),
        400 << 20,
        4 << 20,
        8,
        scratch=[
            pltpu.VMEM((width, width), F32),
            pltpu.VMEM((width, TILE), F32),
            pltpu.VMEM((lanes, width), F32),
            pltpu.VMEM((lanes, rhs), F32),
            pltpu.SemaphoreType.DMA((3,)),
        ],
        in_specs=[SMEM, SMEM, VMEM, VMEM, ANY, ANY, VMEM, ANY] + [VMEM] * len(coupling),
        out_specs=VMEM,
    )(col_at, row_at, yt, l_diag, dl, at, perm_row, v, *coupling)

    if paired:
        blocks = [y_mine] + [swapped(y_mine, "row", row_size, step) for step in range(1, row_size)]
        y_part = call(
            merge_kernel,
            shape(share, columns),
            0,
            1 << 17,
            4,
            in_specs=[SMEM, HBM] + [VMEM] * row_size,
            out_specs=VMEM,
        )(row_at, in_hbm(x), *blocks)
    else:
        y_part = lax.all_gather(y_mine[:, :column_share], "row", axis=1, tiled=True)
    return (y_part, x[:picks, :column_share])


def solution(mesh):
    return jax.shard_map(
        per_device,
        mesh=mesh,
        in_specs=(
            P("row", None),
            P("col", "row"),
            P("col", None),
            P(),
            P(),
            P("col", None),
            P(),
            P("col"),
        ),
        out_specs=(P("col", None), P("col", "row")),
        check_vma=False,
    )
```

```python
import functools

import jax
import jax.numpy as jnp
from jax import lax
from jax.experimental import pallas as pl
from jax.experimental.pallas import tpu as pltpu
from jax.sharding import PartitionSpec as P

F32, BF16 = jnp.float32, jnp.bfloat16
TILE = 128
VMEM = pl.BlockSpec(memory_space=pltpu.VMEM)
SMEM = pl.BlockSpec(memory_space=pltpu.SMEM)
HBM = pl.BlockSpec(memory_space=pltpu.HBM)
ANY = pl.BlockSpec(memory_space=pl.ANY)


def halves(value):
    high = value.astype(BF16)
    return high, (value - high.astype(F32)).astype(BF16)


def mm(left, right):
    return jnp.dot(left, right, preferred_element_type=F32)


def mm_t(left, right):
    return lax.dot_general(left, right, (((1,), (1,)), ((), ())), preferred_element_type=F32)


def dot3(left, right):
    lh, ll = left if isinstance(left, tuple) else halves(left)
    rh, rl = right if isinstance(right, tuple) else halves(right)
    return mm(lh, rh) + (mm(lh, rl) + mm(ll, rh))


def joined(left, right):
    lh, ll = left
    rh, rl = right
    across = jnp.concatenate([jnp.concatenate([rh, rh], axis=0), jnp.concatenate([rl, jnp.zeros_like(rl)], axis=0)], axis=1)
    both = mm(jnp.concatenate([lh, ll], axis=1), across)
    return both[:, : rh.shape[1]] + both[:, rh.shape[1] :]


def tile_of(ref, i, j):
    return ref[i * TILE : (i + 1) * TILE, j * TILE : (j + 1) * TILE]


def iotas():
    shape = (TILE, TILE)
    return lax.broadcasted_iota(jnp.int32, shape, 0), lax.broadcasted_iota(jnp.int32, shape, 1)


def unit_lower_inverses(blocks):
    rows, cols = iotas()
    eye = (rows == cols).astype(F32)
    first = ((rows >> 1) == (cols >> 1)) & (rows > cols)
    found = [eye - jnp.where(first, block, 0.0) for block in blocks]
    pieces = [halves(block) for block in blocks]
    none = jnp.zeros((TILE, TILE), BF16)
    for shift in range(1, TILE.bit_length() - 1):
        off = ((rows >> (shift + 1)) == (cols >> (shift + 1))) & ((rows >> shift) > (cols >> shift))
        parts = [halves(inv) for inv in found]
        mids = [
            halves(joined(part, tuple(jnp.where(off, half, none) for half in piece)))
            for part, piece in zip(parts, pieces)
        ]
        found = [inv - joined(mid, part) for inv, mid, part in zip(found, mids, parts)]
    return found


def started(copies):
    for copy in copies:
        copy.start()
    return copies


def solve_selected_kernel(perm_hbm, lp_hbm, at_ref, perm_ref, tiles_ref, lp_ref, sems):
    width = lp_ref.shape[0]
    count = width // TILE
    spans = [slice(i * TILE, (i + 1) * TILE) for i in range(count)]
    tiles = [pl.ds(i * TILE, TILE) for i in range(count)]
    early = started(
        [pltpu.make_async_copy(lp_hbm.at[tile, tile], tiles_ref.at[tile, :], sems.at[0, i]) for i, tile in enumerate(tiles)]
    )
    late = started(
        [pltpu.make_async_copy(lp_hbm, lp_ref, sems.at[1, 0]), pltpu.make_async_copy(perm_hbm, perm_ref, sems.at[2, 0])]
    )
    for copy in early:
        copy.wait()
    found = unit_lower_inverses([tiles_ref[span, :] for span in spans])
    for copy in late:
        copy.wait()
    perm = perm_ref[...]
    picks = perm.shape[1]
    remain = []
    for i in range(count):
        row_ids = i * TILE + lax.broadcasted_iota(jnp.int32, (TILE, picks), 0)
        remain.append((row_ids == perm).astype(F32))
    for i, span in enumerate(spans):
        value = joined(halves(found[i]), halves(remain[i]))
        solved = halves(value)
        for j in range(i + 1, count):
            remain[j] = remain[j] - joined(halves(tile_of(lp_ref, j, i)), solved)
        at_ref[:, span] = value.T


def invert_upper_kernel(after_ref, u_ref, du_ref):
    del after_ref
    rows, cols = iotas()
    diag = rows == cols
    blocks, scales = [], []
    for i in range(u_ref.shape[0] // TILE):
        upper = tile_of(u_ref, i, i).T
        only = jnp.where(diag, upper, 0.0)
        blocks.append(upper * (1.0 / jnp.sum(only, axis=1, keepdims=True)))
        scales.append(1.0 / jnp.sum(only, axis=0, keepdims=True))
    for i, inv in enumerate(unit_lower_inverses(blocks)):
        du_ref[i * TILE : (i + 1) * TILE, :] = (inv * scales[i]).T


def invert_lower_kernel(after_ref, l_ref, dl_ref):
    del after_ref
    blocks = [tile_of(l_ref, i, i) for i in range(l_ref.shape[0] // TILE)]
    for i, inv in enumerate(unit_lower_inverses(blocks)):
        dl_ref[i * TILE : (i + 1) * TILE, :] = inv


def product_kernel(size, paired, row_ref, at_ref, after_ref, b_ref, u_cols_ref, y_ref, *refs):
    del after_ref
    out_refs, pay_ref = refs[:-1], refs[-1]
    share = b_ref.shape[0]
    chunk = at_ref.shape[1]
    steps = y_ref.shape[0] // chunk
    total = jnp.zeros(b_ref.shape, F32)
    for k in range(steps):
        lh, ll = halves(u_cols_ref[:, k * chunk : (k + 1) * chunk])
        rh, rl = halves(y_ref[k * chunk : (k + 1) * chunk, :])
        if k == steps - 1:
            ah, al = halves(at_ref[...])
            seen = mm(ah, rh) + (mm(ah, rl) + mm(al, rh))
        top = mm(jnp.concatenate([lh, ll], axis=0), rh)
        total = total - (top[:share] + top[share:] + mm(lh, rl))
    row = row_ref[0, 0]
    pay_ref[:share, :] = total
    pay_ref[share:, :] = seen * (row == size - 1).astype(F32)
    if not paired:
        out_refs[0][...] = pay_ref[...]
        return
    columns = b_ref.shape[1] // size
    chips = size // 2
    chip, core = lax.div(row, 2), lax.rem(row, 2)
    for out_ref, side in zip(out_refs, (core, 1 - core)):
        for step in range(chips):
            place = 2 * (chip ^ step) + side
            out_ref[:, step * columns : (step + 1) * columns] = pay_ref[:, aligned_span(place, columns)]
    keep_ref = out_refs[0]
    keep_ref[:share, :columns] = keep_ref[:share, :columns] + b_ref[:, aligned_span(row, columns)]


def aligned_span(place, size):
    return pl.ds(pl.multiple_of(place * size, size), size)


def place_piece(col, inner, outer, share, step, piece, full_ref, columns):
    low, high = lax.rem(col, inner), lax.div(col, inner)
    for turn in range(outer):
        at = (high ^ turn) * inner + (low ^ step)
        full_ref[aligned_span(at, share), columns] = piece[turn * share : (turn + 1) * share, :]


def solve_u_kernel(inner, outer, share, col_ref, after_ref, u_ref, du_any, *refs):
    del after_ref
    piece_refs = refs[:inner]
    yt_ref, y_ref, full_ref, du_ref, sem = refs[inner:]
    copy = pltpu.make_async_copy(du_any, du_ref, sem)
    copy.start()
    col = col_ref[0, 0]
    for step, piece_ref in enumerate(piece_refs):
        place_piece(col, inner, outer, share, step, piece_ref[...], full_ref, slice(None))
    copy.wait()
    count = u_ref.shape[0] // TILE
    solved = []
    for i in range(count):
        span = slice(i * TILE, (i + 1) * TILE)
        remain = full_ref[span, :].T
        for j in range(i):
            remain = remain - joined(solved[j], halves(tile_of(u_ref, j, i)))
        value = joined(halves(remain), halves(du_ref[span, :]))
        yt_ref[:, span] = value
        full_ref[span, :] = value.T
        solved.append(halves(value))
    y_ref[...] = full_ref[aligned_span(col, share), :]


def finish_kernel(inner, outer, share, parts, col_ref, row_ref, yt_ref, l_ref, dl_any, at_any, perm_ref, v_any, *refs):
    side_refs = refs[: 1 if parts == 1 else 2]
    x_ref, lc_ref, dl_ref, at_ref, v_ref, sems = refs[len(side_refs) :]
    copies = started(
        [
            pltpu.make_async_copy(src, dst, sems.at[k])
            for k, (src, dst) in enumerate([(dl_any, dl_ref), (at_any, at_ref), (v_any, v_ref)])
        ]
    )
    row, col = row_ref[0, 0], col_ref[0, 0]
    rows = outer * share
    columns = lc_ref.shape[1] // parts
    chips = max(parts // 2, 1)
    for turn, side_ref in enumerate(side_refs):
        for step in range(chips):
            if parts == 1:
                target = slice(None)
            else:
                target = aligned_span(row ^ (2 * step) ^ turn, columns)
            for piece in range(inner):
                value = side_ref[piece * rows : (piece + 1) * rows, step * columns : (step + 1) * columns]
                place_piece(col, inner, outer, share, piece, value, lc_ref, target)
    for copy in copies:
        copy.wait()
    width = l_ref.shape[0]
    count = width // TILE
    perm = perm_ref[...]
    picks = perm.shape[1]
    solved = {}
    total = None
    for i in reversed(range(count)):
        span = slice(i * TILE, (i + 1) * TILE)
        remain = yt_ref[:, span]
        for j in range(i + 1, count):
            remain = remain - joined(solved[j], halves(tile_of(l_ref, j, i)))
        solved[i] = halves(joined(halves(remain), halves(dl_ref[span, :])))
        row_ids = width + i * TILE + lax.broadcasted_iota(jnp.int32, (TILE, picks), 0)
        select = (row_ids == perm).astype(F32).astype(BF16)
        term = mm(solved[i][0], select) + mm(solved[i][1], select)
        total = term if total is None else total + term
    z = tuple(jnp.concatenate([solved[i][k] for i in range(count)], axis=1) for k in range(2))
    couple = dot3(z, lc_ref[...])
    ch, cl = halves(couple)
    ah, al = halves(at_ref[...])
    total = total - (mm_t(ch, ah) + (mm_t(ch, al) + mm_t(cl, ah)))
    x_ref[...] = total.T + v_ref[...]


def merge_kernel(row_ref, after_ref, *refs):
    del after_ref
    out_ref = refs[-1]
    for step, ref in enumerate(refs[:-1]):
        out_ref[:, aligned_span(row_ref[0, 0] ^ step, ref.shape[1])] = ref[...]


def call(kernel, outs, flops, bytes_accessed, limit, scratch=(), **specs):
    return pl.pallas_call(
        kernel,
        out_shape=outs,
        scratch_shapes=scratch,
        cost_estimate=pl.CostEstimate(flops=flops, bytes_accessed=bytes_accessed, transcendentals=0),
        compiler_params=pltpu.CompilerParams(vmem_limit_bytes=limit << 20),
        **specs,
    )


def shape(*dims):
    return jax.ShapeDtypeStruct(dims, F32)


def in_hbm(array):
    return pltpu.with_memory_space_constraint(array, pltpu.HBM)


def inner_size(size):
    inner = 1
    while inner * inner * 4 <= size and size % (inner * 2) == 0:
        inner *= 2
    return inner


def swapped(value, axis, size, mask):
    return lax.ppermute(value, axis, [(dst ^ mask, dst) for dst in range(size)])


def gather_line(value, axis, size, inner):
    return jnp.concatenate([value] + [swapped(value, axis, size, mask) for mask in range(inner, size, inner)], axis=0)


def gather_pieces(line, axis, size, inner):
    return [line] + [swapped(line, axis, size, mask) for mask in range(1, inner)]


def per_device(y_prev, u_cols, b_panel, u_diag, l_diag, l_coupling, l_prev_diag, perm):
    width = u_diag.shape[0]
    share = u_cols.shape[0]
    row_size, col_size = lax.axis_size("row"), lax.axis_size("col")
    assert row_size & (row_size - 1) == 0 and col_size & (col_size - 1) == 0
    row, col = lax.axis_index("row"), lax.axis_index("col")
    columns = b_panel.shape[1]
    column_share = columns // row_size
    picks = perm.shape[0]
    paired = row_size % 2 == 0 and column_share % TILE == 0
    chips = row_size // 2
    row_at = row.astype(jnp.int32).reshape(1, 1)
    col_at = col.astype(jnp.int32).reshape(1, 1)
    inner = inner_size(col_size)
    outer = col_size // inner

    parts = row_size if paired and width % (row_size * TILE) == 0 else 1
    quarter = width // parts
    line = lax.dynamic_slice_in_dim(l_coupling, lax.rem(row, parts) * quarter, quarter, 1)
    lines = []
    mask = inner
    while mask < col_size:
        line = jnp.concatenate([line, swapped(line, "col", col_size, mask)], axis=0)
        lines.append(line)
        mask *= 2

    perm_row = jnp.pad(perm, (0, max(TILE - picks, 0)), constant_values=-1)[None, :]
    lanes = perm_row.shape[1]
    sent = share + lanes
    at = call(
        solve_selected_kernel,
        shape(lanes, width),
        6 << 30,
        2 << 20,
        8,
        scratch=[
            pltpu.VMEM(perm_row.shape, jnp.int32),
            pltpu.VMEM((width, TILE), F32),
            pltpu.VMEM((width, width), F32),
            pltpu.SemaphoreType.DMA((3, width // TILE)),
        ],
        in_specs=[HBM] * 2,
        out_specs=VMEM,
    )(in_hbm(perm_row), in_hbm(l_prev_diag))
    inverses = lambda kernel, after, matrix: call(
        kernel, shape(width, TILE), 2 << 30, 2 << 20, 8, in_specs=[ANY, VMEM], out_specs=VMEM
    )(after, matrix)
    outs = [shape(sent, columns // 2)] * 2 if paired else [shape(sent, columns)]
    payload = call(
        functools.partial(product_kernel, row_size, paired),
        outs,
        1 << 30,
        10 << 20,
        12,
        scratch=[pltpu.VMEM((sent, columns), F32)],
        in_specs=[SMEM, VMEM, ANY] + [VMEM] * 3,
        out_specs=[VMEM] * len(outs),
    )(row_at, at, lines[0], b_panel, u_cols, y_prev)

    payload, line = lax.optimization_barrier((payload, line))
    if paired:
        keep = payload[0] + swapped(payload[1], "row", row_size, 1)
        keep, line = lax.optimization_barrier((keep, line))
        turn = lambda step: keep[:, step * column_share : (step + 1) * column_share]
        own = turn(0)
        for step in range(1, chips):
            own = own + swapped(turn(step), "row", row_size, 2 * step)
        resid = own[:share]
    else:
        block = lambda array, place: lax.dynamic_slice_in_dim(array, place * column_share, column_share, 1)
        own = block(payload[0], row)
        for step in range(1, row_size):
            own = own + swapped(block(payload[0], row ^ step), "row", row_size, step)
        resid = own[:share] + block(b_panel, row)
    rhs = max(TILE, column_share)
    mine = jnp.concatenate(gather_pieces(line, "col", col_size, inner), axis=0)
    du = inverses(invert_upper_kernel, keep if paired else payload[0], u_diag)
    resid, mine, du = lax.optimization_barrier((resid, mine, du))
    resid = jnp.pad(resid, ((0, 0), (0, rhs - column_share)))
    v = jnp.pad(own[share:], ((0, 0), (0, rhs - column_share)))
    sides = [mine] + [swapped(mine, "row", row_size, 2 * step) for step in range(1, chips if parts > 1 else 1)]
    line = gather_line(resid, "col", col_size, inner)
    dl = inverses(invert_lower_kernel, line, l_diag)
    pieces = gather_pieces(line, "col", col_size, inner)

    yt, y_mine = call(
        functools.partial(solve_u_kernel, inner, outer, share),
        (shape(rhs, width), shape(share, rhs)),
        200 << 20,
        2 << 20,
        8,
        scratch=[pltpu.VMEM((width, rhs), F32), pltpu.VMEM((width, TILE), F32), pltpu.SemaphoreType.DMA],
        in_specs=[SMEM, ANY, VMEM, ANY] + [VMEM] * inner,
        out_specs=[VMEM] * 2,
    )(col_at, dl, u_diag, du, *pieces)

    yt, sides = lax.optimization_barrier((yt, sides))
    mine = jnp.concatenate(sides, axis=1)
    coupling = [mine, swapped(mine, "row", row_size, 1)] if parts > 1 else [mine]
    x = call(
        functools.partial(finish_kernel, inner, outer, share, parts),
        shape(lanes, rhs),
        400 << 20,
        4 << 20,
        8,
        scratch=[
            pltpu.VMEM((width, width), F32),
            pltpu.VMEM((width, TILE), F32),
            pltpu.VMEM((lanes, width), F32),
            pltpu.VMEM((lanes, rhs), F32),
            pltpu.SemaphoreType.DMA((3,)),
        ],
        in_specs=[SMEM, SMEM, VMEM, VMEM, ANY, ANY, VMEM, ANY] + [VMEM] * len(coupling),
        out_specs=VMEM,
    )(col_at, row_at, yt, l_diag, dl, at, perm_row, v, *coupling)

    if paired:
        blocks = [y_mine] + [swapped(y_mine, "row", row_size, step) for step in range(1, row_size)]
        y_part = call(
            merge_kernel,
            shape(share, columns),
            0,
            1 << 17,
            4,
            in_specs=[SMEM, HBM] + [VMEM] * row_size,
            out_specs=VMEM,
        )(row_at, in_hbm(x), *blocks)
    else:
        y_part = lax.all_gather(y_mine[:, :column_share], "row", axis=1, tiled=True)
    return (y_part, x[:picks, :column_share])


def solution(mesh):
    return jax.shard_map(
        per_device,
        mesh=mesh,
        in_specs=(
            P("row", None),
            P("col", "row"),
            P("col", None),
            P(),
            P(),
            P("col", None),
            P(),
            P("col"),
        ),
        out_specs=(P("col", None), P("col", "row")),
        check_vma=False,
    )
```

```python
import functools

import jax
import jax.numpy as jnp
from jax import lax
from jax.experimental import pallas as pl
from jax.experimental.pallas import tpu as pltpu
from jax.sharding import PartitionSpec as P

F32, BF16 = jnp.float32, jnp.bfloat16
TILE = 128
VMEM = pl.BlockSpec(memory_space=pltpu.VMEM)
SMEM = pl.BlockSpec(memory_space=pltpu.SMEM)
HBM = pl.BlockSpec(memory_space=pltpu.HBM)
ANY = pl.BlockSpec(memory_space=pl.ANY)


def halves(value):
    high = value.astype(BF16)
    return high, (value - high.astype(F32)).astype(BF16)


def mm(left, right):
    return jnp.dot(left, right, preferred_element_type=F32)


def mm_t(left, right):
    return lax.dot_general(left, right, (((1,), (1,)), ((), ())), preferred_element_type=F32)


def dot3(left, right):
    lh, ll = left if isinstance(left, tuple) else halves(left)
    rh, rl = right if isinstance(right, tuple) else halves(right)
    return mm(lh, rh) + (mm(lh, rl) + mm(ll, rh))


def joined(left, right):
    lh, ll = left
    rh, rl = right
    across = jnp.concatenate([jnp.concatenate([rh, rh], axis=0), jnp.concatenate([rl, jnp.zeros_like(rl)], axis=0)], axis=1)
    both = mm(jnp.concatenate([lh, ll], axis=1), across)
    return both[:, : rh.shape[1]] + both[:, rh.shape[1] :]


def tile_of(ref, i, j):
    return ref[i * TILE : (i + 1) * TILE, j * TILE : (j + 1) * TILE]


def iotas():
    shape = (TILE, TILE)
    return lax.broadcasted_iota(jnp.int32, shape, 0), lax.broadcasted_iota(jnp.int32, shape, 1)


def unit_lower_inverses(blocks):
    rows, cols = iotas()
    eye = (rows == cols).astype(F32)
    first = ((rows >> 1) == (cols >> 1)) & (rows > cols)
    found = [eye - jnp.where(first, block, 0.0) for block in blocks]
    pieces = [halves(block) for block in blocks]
    none = jnp.zeros((TILE, TILE), BF16)
    for shift in range(1, TILE.bit_length() - 1):
        off = ((rows >> (shift + 1)) == (cols >> (shift + 1))) & ((rows >> shift) > (cols >> shift))
        parts = [halves(inv) for inv in found]
        mids = [
            halves(joined(part, tuple(jnp.where(off, half, none) for half in piece)))
            for part, piece in zip(parts, pieces)
        ]
        found = [inv - joined(mid, part) for inv, mid, part in zip(found, mids, parts)]
    return found


def started(copies):
    for copy in copies:
        copy.start()
    return copies


def solve_selected_kernel(perm_hbm, lp_hbm, at_ref, perm_ref, tiles_ref, lp_ref, sems):
    width = lp_ref.shape[0]
    count = width // TILE
    spans = [slice(i * TILE, (i + 1) * TILE) for i in range(count)]
    tiles = [pl.ds(i * TILE, TILE) for i in range(count)]
    early = started(
        [pltpu.make_async_copy(lp_hbm.at[tile, tile], tiles_ref.at[tile, :], sems.at[0, i]) for i, tile in enumerate(tiles)]
    )
    late = started(
        [pltpu.make_async_copy(lp_hbm, lp_ref, sems.at[1, 0]), pltpu.make_async_copy(perm_hbm, perm_ref, sems.at[2, 0])]
    )
    for copy in early:
        copy.wait()
    found = unit_lower_inverses([tiles_ref[span, :] for span in spans])
    for copy in late:
        copy.wait()
    perm = perm_ref[...]
    picks = perm.shape[1]
    remain = []
    for i in range(count):
        row_ids = i * TILE + lax.broadcasted_iota(jnp.int32, (TILE, picks), 0)
        remain.append((row_ids == perm).astype(F32))
    for i, span in enumerate(spans):
        value = joined(halves(found[i]), halves(remain[i]))
        solved = halves(value)
        for j in range(i + 1, count):
            remain[j] = remain[j] - joined(halves(tile_of(lp_ref, j, i)), solved)
        at_ref[:, span] = value.T


def invert_upper_kernel(after_ref, u_ref, du_ref):
    del after_ref
    rows, cols = iotas()
    diag = rows == cols
    blocks, scales = [], []
    for i in range(u_ref.shape[0] // TILE):
        upper = tile_of(u_ref, i, i).T
        only = jnp.where(diag, upper, 0.0)
        blocks.append(upper * (1.0 / jnp.sum(only, axis=1, keepdims=True)))
        scales.append(1.0 / jnp.sum(only, axis=0, keepdims=True))
    for i, inv in enumerate(unit_lower_inverses(blocks)):
        du_ref[i * TILE : (i + 1) * TILE, :] = (inv * scales[i]).T


def invert_lower_kernel(after_ref, l_ref, dl_ref):
    del after_ref
    blocks = [tile_of(l_ref, i, i) for i in range(l_ref.shape[0] // TILE)]
    for i, inv in enumerate(unit_lower_inverses(blocks)):
        dl_ref[i * TILE : (i + 1) * TILE, :] = inv


def product_kernel(size, paired, row_ref, at_ref, after_ref, b_ref, u_cols_ref, y_ref, *refs):
    del after_ref
    out_refs, pay_ref = refs[:-1], refs[-1]
    share = b_ref.shape[0]
    chunk = at_ref.shape[1]
    steps = y_ref.shape[0] // chunk
    total = jnp.zeros(b_ref.shape, F32)
    for k in range(steps):
        lh, ll = halves(u_cols_ref[:, k * chunk : (k + 1) * chunk])
        rh, rl = halves(y_ref[k * chunk : (k + 1) * chunk, :])
        if k == steps - 1:
            ah, al = halves(at_ref[...])
            seen = mm(ah, rh) + (mm(ah, rl) + mm(al, rh))
        top = mm(jnp.concatenate([lh, ll], axis=0), rh)
        total = total - (top[:share] + top[share:] + mm(lh, rl))
    row = row_ref[0, 0]
    pay_ref[:share, :] = total
    pay_ref[share:, :] = seen * (row == size - 1).astype(F32)
    if not paired:
        out_refs[0][...] = pay_ref[...]
        return
    columns = b_ref.shape[1] // size
    chips = size // 2
    chip, core = lax.div(row, 2), lax.rem(row, 2)
    for out_ref, side in zip(out_refs, (core, 1 - core)):
        for step in range(chips):
            place = 2 * (chip ^ step) + side
            out_ref[:, step * columns : (step + 1) * columns] = pay_ref[:, aligned_span(place, columns)]
    keep_ref = out_refs[0]
    keep_ref[:share, :columns] = keep_ref[:share, :columns] + b_ref[:, aligned_span(row, columns)]


def aligned_span(place, size):
    return pl.ds(pl.multiple_of(place * size, size), size)


def place_piece(col, inner, outer, share, step, piece, full_ref, columns):
    low, high = lax.rem(col, inner), lax.div(col, inner)
    for turn in range(outer):
        at = (high ^ turn) * inner + (low ^ step)
        full_ref[aligned_span(at, share), columns] = piece[turn * share : (turn + 1) * share, :]


def solve_u_kernel(inner, outer, share, col_ref, after_ref, u_ref, du_any, *refs):
    del after_ref
    piece_refs = refs[:inner]
    yt_ref, y_ref, full_ref, du_ref, sem = refs[inner:]
    copy = pltpu.make_async_copy(du_any, du_ref, sem)
    copy.start()
    col = col_ref[0, 0]
    for step, piece_ref in enumerate(piece_refs):
        place_piece(col, inner, outer, share, step, piece_ref[...], full_ref, slice(None))
    copy.wait()
    count = u_ref.shape[0] // TILE
    solved = []
    for i in range(count):
        span = slice(i * TILE, (i + 1) * TILE)
        remain = full_ref[span, :].T
        for j in range(i):
            remain = remain - joined(solved[j], halves(tile_of(u_ref, j, i)))
        value = joined(halves(remain), halves(du_ref[span, :]))
        yt_ref[:, span] = value
        full_ref[span, :] = value.T
        solved.append(halves(value))
    y_ref[...] = full_ref[aligned_span(col, share), :]


def finish_kernel(inner, outer, share, parts, col_ref, row_ref, yt_ref, l_ref, dl_any, at_any, perm_ref, v_any, *refs):
    side_refs = refs[: 1 if parts == 1 else 2]
    x_ref, lc_ref, dl_ref, at_ref, v_ref, sems = refs[len(side_refs) :]
    copies = started(
        [
            pltpu.make_async_copy(src, dst, sems.at[k])
            for k, (src, dst) in enumerate([(dl_any, dl_ref), (at_any, at_ref), (v_any, v_ref)])
        ]
    )
    row, col = row_ref[0, 0], col_ref[0, 0]
    rows = outer * share
    columns = lc_ref.shape[1] // parts
    chips = max(parts // 2, 1)
    for turn, side_ref in enumerate(side_refs):
        for step in range(chips):
            if parts == 1:
                target = slice(None)
            else:
                target = aligned_span(row ^ (2 * step) ^ turn, columns)
            for piece in range(inner):
                value = side_ref[piece * rows : (piece + 1) * rows, step * columns : (step + 1) * columns]
                place_piece(col, inner, outer, share, piece, value, lc_ref, target)
    for copy in copies:
        copy.wait()
    width = l_ref.shape[0]
    count = width // TILE
    perm = perm_ref[...]
    picks = perm.shape[1]
    solved = {}
    total = None
    for i in reversed(range(count)):
        span = slice(i * TILE, (i + 1) * TILE)
        remain = yt_ref[:, span]
        for j in range(i + 1, count):
            remain = remain - joined(solved[j], halves(tile_of(l_ref, j, i)))
        solved[i] = halves(joined(halves(remain), halves(dl_ref[span, :])))
        row_ids = width + i * TILE + lax.broadcasted_iota(jnp.int32, (TILE, picks), 0)
        select = (row_ids == perm).astype(F32).astype(BF16)
        term = mm(solved[i][0], select) + mm(solved[i][1], select)
        total = term if total is None else total + term
    z = tuple(jnp.concatenate([solved[i][k] for i in range(count)], axis=1) for k in range(2))
    couple = dot3(z, lc_ref[...])
    ch, cl = halves(couple)
    ah, al = halves(at_ref[...])
    total = total - (mm_t(ch, ah) + (mm_t(ch, al) + mm_t(cl, ah)))
    x_ref[...] = total.T + v_ref[...]


def merge_kernel(row_ref, after_ref, *refs):
    del after_ref
    out_ref = refs[-1]
    for step, ref in enumerate(refs[:-1]):
        out_ref[:, aligned_span(row_ref[0, 0] ^ step, ref.shape[1])] = ref[...]


def call(kernel, outs, flops, bytes_accessed, limit, scratch=(), **specs):
    return pl.pallas_call(
        kernel,
        out_shape=outs,
        scratch_shapes=scratch,
        cost_estimate=pl.CostEstimate(flops=flops, bytes_accessed=bytes_accessed, transcendentals=0),
        compiler_params=pltpu.CompilerParams(vmem_limit_bytes=limit << 20),
        **specs,
    )


def shape(*dims):
    return jax.ShapeDtypeStruct(dims, F32)


def in_hbm(array):
    return pltpu.with_memory_space_constraint(array, pltpu.HBM)


def inner_size(size):
    inner = 1
    while inner * inner * 4 <= size and size % (inner * 2) == 0:
        inner *= 2
    return inner


def swapped(value, axis, size, mask):
    return lax.ppermute(value, axis, [(dst ^ mask, dst) for dst in range(size)])


def gather_line(value, axis, size, inner):
    return jnp.concatenate([value] + [swapped(value, axis, size, mask) for mask in range(inner, size, inner)], axis=0)


def gather_pieces(line, axis, size, inner):
    return [line] + [swapped(line, axis, size, mask) for mask in range(1, inner)]


def per_device(y_prev, u_cols, b_panel, u_diag, l_diag, l_coupling, l_prev_diag, perm):
    width = u_diag.shape[0]
    share = u_cols.shape[0]
    row_size, col_size = lax.axis_size("row"), lax.axis_size("col")
    assert row_size & (row_size - 1) == 0 and col_size & (col_size - 1) == 0
    row, col = lax.axis_index("row"), lax.axis_index("col")
    columns = b_panel.shape[1]
    column_share = columns // row_size
    picks = perm.shape[0]
    paired = row_size % 2 == 0 and column_share % TILE == 0
    chips = row_size // 2
    row_at = row.astype(jnp.int32).reshape(1, 1)
    col_at = col.astype(jnp.int32).reshape(1, 1)
    inner = inner_size(col_size)
    outer = col_size // inner

    parts = row_size if paired and width % (row_size * TILE) == 0 else 1
    quarter = width // parts
    line = lax.dynamic_slice_in_dim(l_coupling, lax.rem(row, parts) * quarter, quarter, 1)
    lines = []
    mask = inner
    while mask < col_size:
        line = jnp.concatenate([line, swapped(line, "col", col_size, mask)], axis=0)
        lines.append(line)
        mask *= 2

    perm_row = jnp.pad(perm, (0, max(TILE - picks, 0)), constant_values=-1)[None, :]
    lanes = perm_row.shape[1]
    sent = share + lanes
    at = call(
        solve_selected_kernel,
        shape(lanes, width),
        6 << 30,
        2 << 20,
        8,
        scratch=[
            pltpu.VMEM(perm_row.shape, jnp.int32),
            pltpu.VMEM((width, TILE), F32),
            pltpu.VMEM((width, width), F32),
            pltpu.SemaphoreType.DMA((3, width // TILE)),
        ],
        in_specs=[HBM] * 2,
        out_specs=VMEM,
    )(in_hbm(perm_row), in_hbm(l_prev_diag))
    inverses = lambda kernel, after, matrix: call(
        kernel, shape(width, TILE), 2 << 30, 2 << 20, 8, in_specs=[ANY, VMEM], out_specs=VMEM
    )(after, matrix)
    outs = [shape(sent, columns // 2)] * 2 if paired else [shape(sent, columns)]
    payload = call(
        functools.partial(product_kernel, row_size, paired),
        outs,
        1 << 30,
        10 << 20,
        12,
        scratch=[pltpu.VMEM((sent, columns), F32)],
        in_specs=[SMEM, VMEM, ANY] + [VMEM] * 3,
        out_specs=[VMEM] * len(outs),
    )(row_at, at, lines[0], b_panel, u_cols, y_prev)

    payload, line = lax.optimization_barrier((payload, line))
    if paired:
        keep = payload[0] + swapped(payload[1], "row", row_size, 1)
        keep, line = lax.optimization_barrier((keep, line))
        turn = lambda step: keep[:, step * column_share : (step + 1) * column_share]
        own = turn(0)
        for step in range(1, chips):
            own = own + swapped(turn(step), "row", row_size, 2 * step)
        resid = own[:share]
    else:
        block = lambda array, place: lax.dynamic_slice_in_dim(array, place * column_share, column_share, 1)
        own = block(payload[0], row)
        for step in range(1, row_size):
            own = own + swapped(block(payload[0], row ^ step), "row", row_size, step)
        resid = own[:share] + block(b_panel, row)
    rhs = max(TILE, column_share)
    mine = jnp.concatenate(gather_pieces(line, "col", col_size, inner), axis=0)
    du = inverses(invert_upper_kernel, keep if paired else payload[0], u_diag)
    resid, du = lax.optimization_barrier((resid, du))
    resid = jnp.pad(resid, ((0, 0), (0, rhs - column_share)))
    v = jnp.pad(own[share:], ((0, 0), (0, rhs - column_share)))
    sides = [mine] + [swapped(mine, "row", row_size, 2 * step) for step in range(1, chips if parts > 1 else 1)]
    line = gather_line(resid, "col", col_size, inner)
    dl = inverses(invert_lower_kernel, line, l_diag)
    pieces = gather_pieces(line, "col", col_size, inner)

    yt, y_mine = call(
        functools.partial(solve_u_kernel, inner, outer, share),
        (shape(rhs, width), shape(share, rhs)),
        200 << 20,
        2 << 20,
        8,
        scratch=[pltpu.VMEM((width, rhs), F32), pltpu.VMEM((width, TILE), F32), pltpu.SemaphoreType.DMA],
        in_specs=[SMEM, ANY, VMEM, ANY] + [VMEM] * inner,
        out_specs=[VMEM] * 2,
    )(col_at, dl, u_diag, du, *pieces)

    yt, sides = lax.optimization_barrier((yt, sides))
    mine = jnp.concatenate(sides, axis=1)
    coupling = [mine, swapped(mine, "row", row_size, 1)] if parts > 1 else [mine]
    x = call(
        functools.partial(finish_kernel, inner, outer, share, parts),
        shape(lanes, rhs),
        400 << 20,
        4 << 20,
        8,
        scratch=[
            pltpu.VMEM((width, width), F32),
            pltpu.VMEM((width, TILE), F32),
            pltpu.VMEM((lanes, width), F32),
            pltpu.VMEM((lanes, rhs), F32),
            pltpu.SemaphoreType.DMA((3,)),
        ],
        in_specs=[SMEM, SMEM, VMEM, VMEM, ANY, ANY, VMEM, ANY] + [VMEM] * len(coupling),
        out_specs=VMEM,
    )(col_at, row_at, yt, l_diag, dl, at, perm_row, v, *coupling)

    if paired:
        blocks = [y_mine] + [swapped(y_mine, "row", row_size, step) for step in range(1, row_size)]
        y_part = call(
            merge_kernel,
            shape(share, columns),
            0,
            1 << 17,
            4,
            in_specs=[SMEM, HBM] + [VMEM] * row_size,
            out_specs=VMEM,
        )(row_at, in_hbm(x), *blocks)
    else:
        y_part = lax.all_gather(y_mine[:, :column_share], "row", axis=1, tiled=True)
    return (y_part, x[:picks, :column_share])


def solution(mesh):
    return jax.shard_map(
        per_device,
        mesh=mesh,
        in_specs=(
            P("row", None),
            P("col", "row"),
            P("col", None),
            P(),
            P(),
            P("col", None),
            P(),
            P("col"),
        ),
        out_specs=(P("col", None), P("col", "row")),
        check_vma=False,
    )
```

```python
import functools

import jax
import jax.numpy as jnp
from jax import lax
from jax.experimental import pallas as pl
from jax.experimental.pallas import tpu as pltpu
from jax.sharding import PartitionSpec as P

F32, BF16 = jnp.float32, jnp.bfloat16
TILE = 128
VMEM = pl.BlockSpec(memory_space=pltpu.VMEM)
SMEM = pl.BlockSpec(memory_space=pltpu.SMEM)
HBM = pl.BlockSpec(memory_space=pltpu.HBM)
ANY = pl.BlockSpec(memory_space=pl.ANY)


def halves(value):
    high = value.astype(BF16)
    return high, (value - high.astype(F32)).astype(BF16)


def mm(left, right):
    return jnp.dot(left, right, preferred_element_type=F32)


def mm_t(left, right):
    return lax.dot_general(left, right, (((1,), (1,)), ((), ())), preferred_element_type=F32)


def dot3(left, right):
    lh, ll = left if isinstance(left, tuple) else halves(left)
    rh, rl = right if isinstance(right, tuple) else halves(right)
    return mm(lh, rh) + (mm(lh, rl) + mm(ll, rh))


def joined(left, right):
    lh, ll = left
    rh, rl = right
    across = jnp.concatenate([jnp.concatenate([rh, rh], axis=0), jnp.concatenate([rl, jnp.zeros_like(rl)], axis=0)], axis=1)
    both = mm(jnp.concatenate([lh, ll], axis=1), across)
    return both[:, : rh.shape[1]] + both[:, rh.shape[1] :]


def tile_of(ref, i, j):
    return ref[i * TILE : (i + 1) * TILE, j * TILE : (j + 1) * TILE]


def iotas():
    shape = (TILE, TILE)
    return lax.broadcasted_iota(jnp.int32, shape, 0), lax.broadcasted_iota(jnp.int32, shape, 1)


def unit_lower_inverses(blocks):
    rows, cols = iotas()
    eye = (rows == cols).astype(F32)
    first = ((rows >> 1) == (cols >> 1)) & (rows > cols)
    found = [eye - jnp.where(first, block, 0.0) for block in blocks]
    pieces = [halves(block) for block in blocks]
    none = jnp.zeros((TILE, TILE), BF16)
    for shift in range(1, TILE.bit_length() - 1):
        off = ((rows >> (shift + 1)) == (cols >> (shift + 1))) & ((rows >> shift) > (cols >> shift))
        parts = [halves(inv) for inv in found]
        mids = [
            halves(joined(part, tuple(jnp.where(off, half, none) for half in piece)))
            for part, piece in zip(parts, pieces)
        ]
        found = [inv - joined(mid, part) for inv, mid, part in zip(found, mids, parts)]
    return found


def started(copies):
    for copy in copies:
        copy.start()
    return copies


def solve_selected_kernel(perm_hbm, lp_hbm, at_ref, perm_ref, tiles_ref, lp_ref, sems):
    width = lp_ref.shape[0]
    count = width // TILE
    spans = [slice(i * TILE, (i + 1) * TILE) for i in range(count)]
    tiles = [pl.ds(i * TILE, TILE) for i in range(count)]
    early = started(
        [pltpu.make_async_copy(lp_hbm.at[tile, tile], tiles_ref.at[tile, :], sems.at[0, i]) for i, tile in enumerate(tiles)]
    )
    late = started(
        [pltpu.make_async_copy(lp_hbm, lp_ref, sems.at[1, 0]), pltpu.make_async_copy(perm_hbm, perm_ref, sems.at[2, 0])]
    )
    for copy in early:
        copy.wait()
    found = unit_lower_inverses([tiles_ref[span, :] for span in spans])
    for copy in late:
        copy.wait()
    perm = perm_ref[...]
    picks = perm.shape[1]
    remain = []
    for i in range(count):
        row_ids = i * TILE + lax.broadcasted_iota(jnp.int32, (TILE, picks), 0)
        remain.append((row_ids == perm).astype(F32))
    for i, span in enumerate(spans):
        value = joined(halves(found[i]), halves(remain[i]))
        solved = halves(value)
        for j in range(i + 1, count):
            remain[j] = remain[j] - joined(halves(tile_of(lp_ref, j, i)), solved)
        at_ref[:, span] = value.T


def invert_upper_kernel(after_ref, u_ref, du_ref):
    del after_ref
    rows, cols = iotas()
    diag = rows == cols
    blocks, scales = [], []
    for i in range(u_ref.shape[0] // TILE):
        upper = tile_of(u_ref, i, i).T
        only = jnp.where(diag, upper, 0.0)
        blocks.append(upper * (1.0 / jnp.sum(only, axis=1, keepdims=True)))
        scales.append(1.0 / jnp.sum(only, axis=0, keepdims=True))
    for i, inv in enumerate(unit_lower_inverses(blocks)):
        du_ref[i * TILE : (i + 1) * TILE, :] = (inv * scales[i]).T


def invert_lower_kernel(after_ref, l_ref, dl_ref):
    del after_ref
    blocks = [tile_of(l_ref, i, i) for i in range(l_ref.shape[0] // TILE)]
    for i, inv in enumerate(unit_lower_inverses(blocks)):
        dl_ref[i * TILE : (i + 1) * TILE, :] = inv


def product_kernel(size, paired, row_ref, at_ref, after_ref, b_ref, u_cols_ref, y_ref, *refs):
    del after_ref
    out_refs, pay_ref = refs[:-1], refs[-1]
    share = b_ref.shape[0]
    chunk = at_ref.shape[1]
    steps = y_ref.shape[0] // chunk
    total = jnp.zeros(b_ref.shape, F32)
    for k in range(steps):
        lh, ll = halves(u_cols_ref[:, k * chunk : (k + 1) * chunk])
        rh, rl = halves(y_ref[k * chunk : (k + 1) * chunk, :])
        if k == steps - 1:
            ah, al = halves(at_ref[...])
            seen = mm(ah, rh) + (mm(ah, rl) + mm(al, rh))
        top = mm(jnp.concatenate([lh, ll], axis=0), rh)
        total = total - (top[:share] + top[share:] + mm(lh, rl))
    row = row_ref[0, 0]
    pay_ref[:share, :] = total
    pay_ref[share:, :] = seen * (row == size - 1).astype(F32)
    if not paired:
        out_refs[0][...] = pay_ref[...]
        return
    columns = b_ref.shape[1] // size
    chips = size // 2
    chip, core = lax.div(row, 2), lax.rem(row, 2)
    for out_ref, side in zip(out_refs, (core, 1 - core)):
        for step in range(chips):
            place = 2 * (chip ^ step) + side
            out_ref[:, step * columns : (step + 1) * columns] = pay_ref[:, aligned_span(place, columns)]
    keep_ref = out_refs[0]
    keep_ref[:share, :columns] = keep_ref[:share, :columns] + b_ref[:, aligned_span(row, columns)]


def aligned_span(place, size):
    return pl.ds(pl.multiple_of(place * size, size), size)


def place_piece(col, inner, outer, share, step, piece, full_ref, columns, down=False):
    low, high = lax.rem(col, inner), lax.div(col, inner)
    for turn in range(outer):
        at = (high ^ ((outer - turn) % outer if down else turn)) * inner + (low ^ step)
        full_ref[aligned_span(at, share), columns] = piece[turn * share : (turn + 1) * share, :]


def solve_u_kernel(inner, outer, share, col_ref, after_ref, u_ref, du_ref, *refs):
    del after_ref
    piece_refs = refs[:inner]
    yt_ref, y_ref, full_ref = refs[inner:]
    col = col_ref[0, 0]
    for step, piece_ref in enumerate(piece_refs):
        place_piece(col, inner, outer, share, step, piece_ref[...], full_ref, slice(None), True)
    count = u_ref.shape[0] // TILE
    solved = []
    for i in range(count):
        span = slice(i * TILE, (i + 1) * TILE)
        remain = full_ref[span, :].T
        for j in range(i):
            remain = remain - joined(solved[j], halves(tile_of(u_ref, j, i)))
        value = joined(halves(remain), halves(du_ref[span, :]))
        yt_ref[:, span] = value
        full_ref[span, :] = value.T
        solved.append(halves(value))
    y_ref[...] = full_ref[aligned_span(col, share), :]


def finish_kernel(inner, outer, share, parts, col_ref, row_ref, yt_ref, l_ref, dl_ref, at_ref, perm_ref, v_ref, *refs):
    side_refs = refs[: 1 if parts == 1 else 2]
    x_ref, lc_ref = refs[len(side_refs) :]
    row, col = row_ref[0, 0], col_ref[0, 0]
    rows = outer * share
    columns = lc_ref.shape[1] // parts
    chips = max(parts // 2, 1)
    for turn, side_ref in enumerate(side_refs):
        for step in range(chips):
            if parts == 1:
                target = slice(None)
            else:
                target = aligned_span(row ^ (2 * step) ^ turn, columns)
            for piece in range(inner):
                value = side_ref[piece * rows : (piece + 1) * rows, step * columns : (step + 1) * columns]
                place_piece(col, inner, outer, share, piece, value, lc_ref, target)
    width = l_ref.shape[0]
    count = width // TILE
    perm = perm_ref[...]
    picks = perm.shape[1]
    solved = {}
    total = None
    for i in reversed(range(count)):
        span = slice(i * TILE, (i + 1) * TILE)
        remain = yt_ref[:, span]
        for j in range(i + 1, count):
            remain = remain - joined(solved[j], halves(tile_of(l_ref, j, i)))
        solved[i] = halves(joined(halves(remain), halves(dl_ref[span, :])))
        row_ids = width + i * TILE + lax.broadcasted_iota(jnp.int32, (TILE, picks), 0)
        select = (row_ids == perm).astype(F32).astype(BF16)
        term = mm(solved[i][0], select) + mm(solved[i][1], select)
        total = term if total is None else total + term
    z = tuple(jnp.concatenate([solved[i][k] for i in range(count)], axis=1) for k in range(2))
    couple = dot3(z, lc_ref[...])
    ch, cl = halves(couple)
    ah, al = halves(at_ref[...])
    total = total - (mm_t(ch, ah) + (mm_t(ch, al) + mm_t(cl, ah)))
    x_ref[...] = total.T + v_ref[...]


def merge_kernel(row_ref, after_ref, *refs):
    del after_ref
    out_ref = refs[-1]
    for step, ref in enumerate(refs[:-1]):
        out_ref[:, aligned_span(row_ref[0, 0] ^ ((len(refs) - 1 - step) % (len(refs) - 1)), ref.shape[1])] = ref[...]


def call(kernel, outs, flops, bytes_accessed, limit, scratch=(), **specs):
    return pl.pallas_call(
        kernel,
        out_shape=outs,
        scratch_shapes=scratch,
        cost_estimate=pl.CostEstimate(flops=flops, bytes_accessed=bytes_accessed, transcendentals=0),
        compiler_params=pltpu.CompilerParams(vmem_limit_bytes=limit << 20),
        **specs,
    )


def shape(*dims):
    return jax.ShapeDtypeStruct(dims, F32)


def in_hbm(array):
    return pltpu.with_memory_space_constraint(array, pltpu.HBM)


def inner_size(size):
    inner = 1
    while inner * inner * 4 <= size and size % (inner * 2) == 0:
        inner *= 2
    return inner


def swapped(value, axis, size, mask):
    return lax.ppermute(value, axis, [(dst ^ mask, dst) for dst in range(size)])


def gather_line(value, axis, size, inner):
    return jnp.concatenate([value] + [swapped(value, axis, size, mask) for mask in range(size - inner, 0, -inner)], axis=0)


def gather_pieces(line, axis, size, inner):
    return [line] + [swapped(line, axis, size, mask) for mask in range(1, inner)]


def per_device(y_prev, u_cols, b_panel, u_diag, l_diag, l_coupling, l_prev_diag, perm):
    width = u_diag.shape[0]
    share = u_cols.shape[0]
    row_size, col_size = lax.axis_size("row"), lax.axis_size("col")
    assert row_size & (row_size - 1) == 0 and col_size & (col_size - 1) == 0
    row, col = lax.axis_index("row"), lax.axis_index("col")
    columns = b_panel.shape[1]
    column_share = columns // row_size
    picks = perm.shape[0]
    paired = row_size % 2 == 0 and column_share % TILE == 0
    chips = row_size // 2
    row_at = row.astype(jnp.int32).reshape(1, 1)
    col_at = col.astype(jnp.int32).reshape(1, 1)
    inner = inner_size(col_size)
    outer = col_size // inner

    parts = row_size if paired and width % (row_size * TILE) == 0 else 1
    quarter = width // parts
    line = lax.dynamic_slice_in_dim(l_coupling, lax.rem(row, parts) * quarter, quarter, 1)
    lines = []
    mask = inner
    while mask < col_size:
        line = jnp.concatenate([line, swapped(line, "col", col_size, mask)], axis=0)
        lines.append(line)
        mask *= 2

    perm_row = jnp.pad(perm, (0, max(TILE - picks, 0)), constant_values=-1)[None, :]
    lanes = perm_row.shape[1]
    sent = share + lanes
    at = call(
        solve_selected_kernel,
        shape(lanes, width),
        6 << 30,
        2 << 20,
        8,
        scratch=[
            pltpu.VMEM(perm_row.shape, jnp.int32),
            pltpu.VMEM((width, TILE), F32),
            pltpu.VMEM((width, width), F32),
            pltpu.SemaphoreType.DMA((3, width // TILE)),
        ],
        in_specs=[HBM] * 2,
        out_specs=VMEM,
    )(in_hbm(perm_row), in_hbm(l_prev_diag))
    inverses = lambda kernel, after, matrix: call(
        kernel, shape(width, TILE), 2 << 30, 2 << 20, 8, in_specs=[ANY, VMEM], out_specs=VMEM
    )(after, matrix)
    outs = [shape(sent, columns // 2)] * 2 if paired else [shape(sent, columns)]
    payload = call(
        functools.partial(product_kernel, row_size, paired),
        outs,
        1 << 30,
        10 << 20,
        12,
        scratch=[pltpu.VMEM((sent, columns), F32)],
        in_specs=[SMEM, VMEM, ANY] + [VMEM] * 3,
        out_specs=[VMEM] * len(outs),
    )(row_at, at, lines[0], b_panel, u_cols, y_prev)

    payload, line = lax.optimization_barrier((payload, line))
    if paired:
        keep = payload[0] + swapped(payload[1], "row", row_size, 1)
        keep, line = lax.optimization_barrier((keep, line))
        turn = lambda step: keep[:, step * column_share : (step + 1) * column_share]
        own = turn(0)
        for step in range(1, chips):
            own = own + swapped(turn(step), "row", row_size, 2 * step)
        resid = own[:share]
    else:
        block = lambda array, place: lax.dynamic_slice_in_dim(array, place * column_share, column_share, 1)
        own = block(payload[0], row)
        for step in range(1, row_size):
            own = own + swapped(block(payload[0], row ^ step), "row", row_size, step)
        resid = own[:share] + block(b_panel, row)
    rhs = max(TILE, column_share)
    mine = jnp.concatenate(gather_pieces(line, "col", col_size, inner), axis=0)
    du = inverses(invert_upper_kernel, keep if paired else payload[0], u_diag)
    resid, du = lax.optimization_barrier((resid, du))
    resid = jnp.pad(resid, ((0, 0), (0, rhs - column_share)))
    v = jnp.pad(own[share:], ((0, 0), (0, rhs - column_share)))
    sides = [mine] + [swapped(mine, "row", row_size, 2 * step) for step in range(1, chips if parts > 1 else 1)]
    line = gather_line(resid, "col", col_size, inner)
    dl = inverses(invert_lower_kernel, line, l_diag)
    pieces = gather_pieces(line, "col", col_size, inner)

    yt, y_mine = call(
        functools.partial(solve_u_kernel, inner, outer, share),
        (shape(rhs, width), shape(share, rhs)),
        200 << 20,
        2 << 20,
        8,
        scratch=[pltpu.VMEM((width, rhs), F32)],
        in_specs=[SMEM, ANY, VMEM, VMEM] + [VMEM] * inner,
        out_specs=[VMEM] * 2,
    )(col_at, dl, u_diag, du, *pieces)

    yt, sides = lax.optimization_barrier((yt, sides))
    mine = jnp.concatenate(sides, axis=1)
    coupling = [mine, swapped(mine, "row", row_size, 1)] if parts > 1 else [mine]
    x = call(
        functools.partial(finish_kernel, inner, outer, share, parts),
        shape(lanes, rhs),
        400 << 20,
        4 << 20,
        8,
        scratch=[
            pltpu.VMEM((width, width), F32),
        ],
        in_specs=[SMEM, SMEM] + [VMEM] * 6 + [VMEM] * len(coupling),
        out_specs=VMEM,
    )(col_at, row_at, yt, l_diag, dl, at, perm_row, v, *coupling)

    if paired:
        blocks = [y_mine] + [swapped(y_mine, "row", row_size, step) for step in range(row_size - 1, 0, -1)]
        y_part = call(
            merge_kernel,
            shape(share, columns),
            0,
            1 << 17,
            4,
            in_specs=[SMEM, HBM] + [VMEM] * row_size,
            out_specs=VMEM,
        )(row_at, in_hbm(x), *blocks)
    else:
        y_part = lax.all_gather(y_mine[:, :column_share], "row", axis=1, tiled=True)
    return (y_part, x[:picks, :column_share])


def solution(mesh):
    return jax.shard_map(
        per_device,
        mesh=mesh,
        in_specs=(
            P("row", None),
            P("col", "row"),
            P("col", None),
            P(),
            P(),
            P("col", None),
            P(),
            P("col"),
        ),
        out_specs=(P("col", None), P("col", "row")),
        check_vma=False,
    )
```

```python
import functools

import jax
import jax.numpy as jnp
from jax import lax
from jax.experimental import pallas as pl
from jax.experimental.pallas import tpu as pltpu
from jax.sharding import PartitionSpec as P

F32, BF16 = jnp.float32, jnp.bfloat16
TILE = 128
VMEM = pl.BlockSpec(memory_space=pltpu.VMEM)
SMEM = pl.BlockSpec(memory_space=pltpu.SMEM)
HBM = pl.BlockSpec(memory_space=pltpu.HBM)
ANY = pl.BlockSpec(memory_space=pl.ANY)


def halves(value):
    high = value.astype(BF16)
    return high, (value - high.astype(F32)).astype(BF16)


def mm(left, right):
    return jnp.dot(left, right, preferred_element_type=F32)


def mm_t(left, right):
    return lax.dot_general(left, right, (((1,), (1,)), ((), ())), preferred_element_type=F32)


def dot3(left, right):
    lh, ll = left if isinstance(left, tuple) else halves(left)
    rh, rl = right if isinstance(right, tuple) else halves(right)
    return mm(lh, rh) + (mm(lh, rl) + mm(ll, rh))


def joined(left, right):
    lh, ll = left
    rh, rl = right
    across = jnp.concatenate([jnp.concatenate([rh, rh], axis=0), jnp.concatenate([rl, jnp.zeros_like(rl)], axis=0)], axis=1)
    both = mm(jnp.concatenate([lh, ll], axis=1), across)
    return both[:, : rh.shape[1]] + both[:, rh.shape[1] :]


def tile_of(ref, i, j):
    return ref[i * TILE : (i + 1) * TILE, j * TILE : (j + 1) * TILE]


def iotas():
    shape = (TILE, TILE)
    return lax.broadcasted_iota(jnp.int32, shape, 0), lax.broadcasted_iota(jnp.int32, shape, 1)


def unit_lower_inverses(blocks):
    rows, cols = iotas()
    eye = (rows == cols).astype(F32)
    first = ((rows >> 1) == (cols >> 1)) & (rows > cols)
    found = [eye - jnp.where(first, block, 0.0) for block in blocks]
    pieces = [halves(block) for block in blocks]
    none = jnp.zeros((TILE, TILE), BF16)
    for shift in range(1, TILE.bit_length() - 1):
        off = ((rows >> (shift + 1)) == (cols >> (shift + 1))) & ((rows >> shift) > (cols >> shift))
        parts = [halves(inv) for inv in found]
        mids = [
            halves(joined(part, tuple(jnp.where(off, half, none) for half in piece)))
            for part, piece in zip(parts, pieces)
        ]
        found = [inv - joined(mid, part) for inv, mid, part in zip(found, mids, parts)]
    return found


def started(copies):
    for copy in copies:
        copy.start()
    return copies


def solve_selected_kernel(perm_hbm, lp_hbm, at_ref, perm_ref, tiles_ref, lp_ref, sems):
    width = lp_ref.shape[0]
    count = width // TILE
    spans = [slice(i * TILE, (i + 1) * TILE) for i in range(count)]
    tiles = [pl.ds(i * TILE, TILE) for i in range(count)]
    early = started(
        [pltpu.make_async_copy(lp_hbm.at[tile, tile], tiles_ref.at[tile, :], sems.at[0, i]) for i, tile in enumerate(tiles)]
    )
    late = started(
        [pltpu.make_async_copy(lp_hbm, lp_ref, sems.at[1, 0]), pltpu.make_async_copy(perm_hbm, perm_ref, sems.at[2, 0])]
    )
    for copy in early:
        copy.wait()
    found = unit_lower_inverses([tiles_ref[span, :] for span in spans])
    for copy in late:
        copy.wait()
    perm = perm_ref[...]
    picks = perm.shape[1]
    remain = []
    for i in range(count):
        row_ids = i * TILE + lax.broadcasted_iota(jnp.int32, (TILE, picks), 0)
        remain.append((row_ids == perm).astype(F32))
    for i, span in enumerate(spans):
        value = joined(halves(found[i]), halves(remain[i]))
        solved = halves(value)
        for j in range(i + 1, count):
            remain[j] = remain[j] - joined(halves(tile_of(lp_ref, j, i)), solved)
        at_ref[:, span] = value.T


def invert_upper_kernel(after_ref, u_ref, du_ref):
    del after_ref
    rows, cols = iotas()
    diag = rows == cols
    blocks, scales = [], []
    for i in range(u_ref.shape[0] // TILE):
        upper = tile_of(u_ref, i, i).T
        only = jnp.where(diag, upper, 0.0)
        blocks.append(upper * (1.0 / jnp.sum(only, axis=1, keepdims=True)))
        scales.append(1.0 / jnp.sum(only, axis=0, keepdims=True))
    for i, inv in enumerate(unit_lower_inverses(blocks)):
        du_ref[i * TILE : (i + 1) * TILE, :] = (inv * scales[i]).T


def invert_lower_kernel(after_ref, l_ref, dl_ref):
    del after_ref
    blocks = [tile_of(l_ref, i, i) for i in range(l_ref.shape[0] // TILE)]
    for i, inv in enumerate(unit_lower_inverses(blocks)):
        dl_ref[i * TILE : (i + 1) * TILE, :] = inv


def product_kernel(size, paired, row_ref, at_ref, after_ref, b_ref, u_cols_ref, y_ref, *refs):
    del after_ref
    out_refs, pay_ref = refs[:-1], refs[-1]
    share = b_ref.shape[0]
    chunk = at_ref.shape[1]
    steps = y_ref.shape[0] // chunk
    total = jnp.zeros(b_ref.shape, F32)
    for k in range(steps):
        lh, ll = halves(u_cols_ref[:, k * chunk : (k + 1) * chunk])
        rh, rl = halves(y_ref[k * chunk : (k + 1) * chunk, :])
        if k == steps - 1:
            ah, al = halves(at_ref[...])
            seen = mm(ah, rh) + (mm(ah, rl) + mm(al, rh))
        top = mm(jnp.concatenate([lh, ll], axis=0), rh)
        total = total - (top[:share] + top[share:] + mm(lh, rl))
    row = row_ref[0, 0]
    pay_ref[:share, :] = total
    pay_ref[share:, :] = seen * (row == size - 1).astype(F32)
    if not paired:
        out_refs[0][...] = pay_ref[...]
        return
    columns = b_ref.shape[1] // size
    chips = size // 2
    chip, core = lax.div(row, 2), lax.rem(row, 2)
    for out_ref, side in zip(out_refs, (core, 1 - core)):
        for step in range(chips):
            place = 2 * (chip ^ step) + side
            out_ref[:, step * columns : (step + 1) * columns] = pay_ref[:, aligned_span(place, columns)]
    keep_ref = out_refs[0]
    keep_ref[:share, :columns] = keep_ref[:share, :columns] + b_ref[:, aligned_span(row, columns)]


def aligned_span(place, size):
    return pl.ds(pl.multiple_of(place * size, size), size)


def doubled(size):
    order = [0]
    for bit in reversed(range(size.bit_length() - 1)):
        order += [far ^ (1 << bit) for far in order]
    return order


def place_piece(col, inner, order, share, step, piece, full_ref, columns):
    low, high = lax.rem(col, inner), lax.div(col, inner)
    for turn, far in enumerate(order):
        at = (high ^ far) * inner + (low ^ step)
        full_ref[aligned_span(at, share), columns] = piece[turn * share : (turn + 1) * share, :]


def solve_u_kernel(inner, outer, share, col_ref, after_ref, u_ref, du_ref, *refs):
    del after_ref
    piece_refs = refs[:inner]
    yt_ref, y_ref, full_ref = refs[inner:]
    col = col_ref[0, 0]
    for step, piece_ref in enumerate(piece_refs):
        place_piece(col, inner, [0, *range(outer - 1, 0, -1)], share, step, piece_ref[...], full_ref, slice(None))
    count = u_ref.shape[0] // TILE
    solved = []
    for i in range(count):
        span = slice(i * TILE, (i + 1) * TILE)
        remain = full_ref[span, :].T
        for j in range(i):
            remain = remain - joined(solved[j], halves(tile_of(u_ref, j, i)))
        value = joined(halves(remain), halves(du_ref[span, :]))
        yt_ref[:, span] = value
        full_ref[span, :] = value.T
        solved.append(halves(value))
    y_ref[...] = full_ref[aligned_span(col, share), :]


def finish_kernel(inner, outer, share, parts, col_ref, row_ref, yt_ref, l_ref, dl_ref, at_ref, perm_ref, v_ref, *refs):
    side_refs = refs[: 1 if parts == 1 else 2]
    x_ref, lc_ref = refs[len(side_refs) :]
    row, col = row_ref[0, 0], col_ref[0, 0]
    rows = outer * share
    order = doubled(outer)
    columns = lc_ref.shape[1] // parts
    chips = max(parts // 2, 1)
    for turn, side_ref in enumerate(side_refs):
        for step in range(chips):
            if parts == 1:
                target = slice(None)
            else:
                target = aligned_span(row ^ (2 * step) ^ turn, columns)
            for piece in range(inner):
                value = side_ref[piece * rows : (piece + 1) * rows, step * columns : (step + 1) * columns]
                place_piece(col, inner, order, share, piece, value, lc_ref, target)
    width = l_ref.shape[0]
    count = width // TILE
    perm = perm_ref[...]
    picks = perm.shape[1]
    solved = {}
    total = None
    for i in reversed(range(count)):
        span = slice(i * TILE, (i + 1) * TILE)
        remain = yt_ref[:, span]
        for j in range(i + 1, count):
            remain = remain - joined(solved[j], halves(tile_of(l_ref, j, i)))
        solved[i] = halves(joined(halves(remain), halves(dl_ref[span, :])))
        row_ids = width + i * TILE + lax.broadcasted_iota(jnp.int32, (TILE, picks), 0)
        select = (row_ids == perm).astype(F32).astype(BF16)
        term = mm(solved[i][0], select) + mm(solved[i][1], select)
        total = term if total is None else total + term
    z = tuple(jnp.concatenate([solved[i][k] for i in range(count)], axis=1) for k in range(2))
    couple = dot3(z, lc_ref[...])
    ch, cl = halves(couple)
    ah, al = halves(at_ref[...])
    total = total - (mm_t(ch, ah) + (mm_t(ch, al) + mm_t(cl, ah)))
    x_ref[...] = total.T + v_ref[...]


def merge_kernel(row_ref, after_ref, *refs):
    del after_ref
    out_ref = refs[-1]
    for step, ref in enumerate(refs[:-1]):
        out_ref[:, aligned_span(row_ref[0, 0] ^ ((len(refs) - 1 - step) % (len(refs) - 1)), ref.shape[1])] = ref[...]


def call(kernel, outs, flops, bytes_accessed, limit, scratch=(), **specs):
    return pl.pallas_call(
        kernel,
        out_shape=outs,
        scratch_shapes=scratch,
        cost_estimate=pl.CostEstimate(flops=flops, bytes_accessed=bytes_accessed, transcendentals=0),
        compiler_params=pltpu.CompilerParams(vmem_limit_bytes=limit << 20),
        **specs,
    )


def shape(*dims):
    return jax.ShapeDtypeStruct(dims, F32)


def in_hbm(array):
    return pltpu.with_memory_space_constraint(array, pltpu.HBM)


def inner_size(size):
    inner = 1
    while inner * inner * 4 <= size and size % (inner * 2) == 0:
        inner *= 2
    return inner


def swapped(value, axis, size, mask):
    return lax.ppermute(value, axis, [(dst ^ mask, dst) for dst in range(size)])


def gather_line(value, axis, size, inner):
    return jnp.concatenate([value] + [swapped(value, axis, size, mask) for mask in range(size - inner, 0, -inner)], axis=0)


def gather_pieces(line, axis, size, inner):
    return [line] + [swapped(line, axis, size, mask) for mask in range(1, inner)]


def per_device(y_prev, u_cols, b_panel, u_diag, l_diag, l_coupling, l_prev_diag, perm):
    width = u_diag.shape[0]
    share = u_cols.shape[0]
    row_size, col_size = lax.axis_size("row"), lax.axis_size("col")
    assert row_size & (row_size - 1) == 0 and col_size & (col_size - 1) == 0
    row, col = lax.axis_index("row"), lax.axis_index("col")
    columns = b_panel.shape[1]
    column_share = columns // row_size
    picks = perm.shape[0]
    paired = row_size % 2 == 0 and column_share % TILE == 0
    chips = row_size // 2
    row_at = row.astype(jnp.int32).reshape(1, 1)
    col_at = col.astype(jnp.int32).reshape(1, 1)
    inner = inner_size(col_size)
    outer = col_size // inner

    parts = row_size if paired and width % (row_size * TILE) == 0 else 1
    quarter = width // parts
    line = lax.dynamic_slice_in_dim(l_coupling, lax.rem(row, parts) * quarter, quarter, 1)
    lines = []
    mask = col_size // 2
    while mask >= inner:
        line = jnp.concatenate([line, swapped(line, "col", col_size, mask)], axis=0)
        lines.append(line)
        mask //= 2

    perm_row = jnp.pad(perm, (0, max(TILE - picks, 0)), constant_values=-1)[None, :]
    lanes = perm_row.shape[1]
    sent = share + lanes
    at = call(
        solve_selected_kernel,
        shape(lanes, width),
        6 << 30,
        2 << 20,
        8,
        scratch=[
            pltpu.VMEM(perm_row.shape, jnp.int32),
            pltpu.VMEM((width, TILE), F32),
            pltpu.VMEM((width, width), F32),
            pltpu.SemaphoreType.DMA((3, width // TILE)),
        ],
        in_specs=[HBM] * 2,
        out_specs=VMEM,
    )(in_hbm(perm_row), in_hbm(l_prev_diag))
    inverses = lambda kernel, after, matrix: call(
        kernel, shape(width, TILE), 2 << 30, 2 << 20, 8, in_specs=[ANY, VMEM], out_specs=VMEM
    )(after, matrix)
    outs = [shape(sent, columns // 2)] * 2 if paired else [shape(sent, columns)]
    payload = call(
        functools.partial(product_kernel, row_size, paired),
        outs,
        1 << 30,
        10 << 20,
        12,
        scratch=[pltpu.VMEM((sent, columns), F32)],
        in_specs=[SMEM, VMEM, ANY] + [VMEM] * 3,
        out_specs=[VMEM] * len(outs),
    )(row_at, at, lines[0], b_panel, u_cols, y_prev)

    payload, line = lax.optimization_barrier((payload, line))
    if paired:
        keep = payload[0] + swapped(payload[1], "row", row_size, 1)
        keep, line = lax.optimization_barrier((keep, line))
        turn = lambda step: keep[:, step * column_share : (step + 1) * column_share]
        own = turn(0)
        for step in range(1, chips):
            own = own + swapped(turn(step), "row", row_size, 2 * step)
        resid = own[:share]
    else:
        block = lambda array, place: lax.dynamic_slice_in_dim(array, place * column_share, column_share, 1)
        own = block(payload[0], row)
        for step in range(1, row_size):
            own = own + swapped(block(payload[0], row ^ step), "row", row_size, step)
        resid = own[:share] + block(b_panel, row)
    rhs = max(TILE, column_share)
    mine = jnp.concatenate(gather_pieces(line, "col", col_size, inner), axis=0)
    du = inverses(invert_upper_kernel, keep if paired else payload[0], u_diag)
    resid, du = lax.optimization_barrier((resid, du))
    resid = jnp.pad(resid, ((0, 0), (0, rhs - column_share)))
    v = jnp.pad(own[share:], ((0, 0), (0, rhs - column_share)))
    sides = [mine] + [swapped(mine, "row", row_size, 2 * step) for step in range(1, chips if parts > 1 else 1)]
    line = gather_line(resid, "col", col_size, inner)
    dl = inverses(invert_lower_kernel, line, l_diag)
    pieces = gather_pieces(line, "col", col_size, inner)

    yt, y_mine = call(
        functools.partial(solve_u_kernel, inner, outer, share),
        (shape(rhs, width), shape(share, rhs)),
        200 << 20,
        2 << 20,
        8,
        scratch=[pltpu.VMEM((width, rhs), F32)],
        in_specs=[SMEM, ANY, VMEM, VMEM] + [VMEM] * inner,
        out_specs=[VMEM] * 2,
    )(col_at, dl, u_diag, du, *pieces)

    yt, sides = lax.optimization_barrier((yt, sides))
    mine = jnp.concatenate(sides, axis=1)
    coupling = [mine, swapped(mine, "row", row_size, 1)] if parts > 1 else [mine]
    x = call(
        functools.partial(finish_kernel, inner, outer, share, parts),
        shape(lanes, rhs),
        400 << 20,
        4 << 20,
        8,
        scratch=[
            pltpu.VMEM((width, width), F32),
        ],
        in_specs=[SMEM, SMEM] + [VMEM] * 6 + [VMEM] * len(coupling),
        out_specs=VMEM,
    )(col_at, row_at, yt, l_diag, dl, at, perm_row, v, *coupling)

    if paired:
        blocks = [y_mine] + [swapped(y_mine, "row", row_size, step) for step in range(row_size - 1, 0, -1)]
        y_part = call(
            merge_kernel,
            shape(share, columns),
            0,
            1 << 17,
            4,
            in_specs=[SMEM, HBM] + [VMEM] * row_size,
            out_specs=VMEM,
        )(row_at, in_hbm(x), *blocks)
    else:
        y_part = lax.all_gather(y_mine[:, :column_share], "row", axis=1, tiled=True)
    return (y_part, x[:picks, :column_share])


def solution(mesh):
    return jax.shard_map(
        per_device,
        mesh=mesh,
        in_specs=(
            P("row", None),
            P("col", "row"),
            P("col", None),
            P(),
            P(),
            P("col", None),
            P(),
            P("col"),
        ),
        out_specs=(P("col", None), P("col", "row")),
        check_vma=False,
    )
```

```python
import functools

import jax
import jax.numpy as jnp
from jax import lax
from jax.experimental import pallas as pl
from jax.experimental.pallas import tpu as pltpu
from jax.sharding import PartitionSpec as P

F32, BF16 = jnp.float32, jnp.bfloat16
TILE = 128
VMEM = pl.BlockSpec(memory_space=pltpu.VMEM)
SMEM = pl.BlockSpec(memory_space=pltpu.SMEM)
HBM = pl.BlockSpec(memory_space=pltpu.HBM)
ANY = pl.BlockSpec(memory_space=pl.ANY)


def halves(value):
    high = value.astype(BF16)
    return high, (value - high.astype(F32)).astype(BF16)


def mm(left, right):
    return jnp.dot(left, right, preferred_element_type=F32)


def mm_t(left, right):
    return lax.dot_general(left, right, (((1,), (1,)), ((), ())), preferred_element_type=F32)


def dot3(left, right):
    lh, ll = left if isinstance(left, tuple) else halves(left)
    rh, rl = right if isinstance(right, tuple) else halves(right)
    return mm(lh, rh) + (mm(lh, rl) + mm(ll, rh))


def joined(left, right):
    lh, ll = left
    rh, rl = right
    across = jnp.concatenate([jnp.concatenate([rh, rh], axis=0), jnp.concatenate([rl, jnp.zeros_like(rl)], axis=0)], axis=1)
    both = mm(jnp.concatenate([lh, ll], axis=1), across)
    return both[:, : rh.shape[1]] + both[:, rh.shape[1] :]


def tile_of(ref, i, j):
    return ref[i * TILE : (i + 1) * TILE, j * TILE : (j + 1) * TILE]


def iotas():
    shape = (TILE, TILE)
    return lax.broadcasted_iota(jnp.int32, shape, 0), lax.broadcasted_iota(jnp.int32, shape, 1)


def unit_lower_inverses(blocks):
    rows, cols = iotas()
    eye = (rows == cols).astype(F32)
    first = ((rows >> 1) == (cols >> 1)) & (rows > cols)
    found = [eye - jnp.where(first, block, 0.0) for block in blocks]
    pieces = [halves(block) for block in blocks]
    none = jnp.zeros((TILE, TILE), BF16)
    for shift in range(1, TILE.bit_length() - 1):
        off = ((rows >> (shift + 1)) == (cols >> (shift + 1))) & ((rows >> shift) > (cols >> shift))
        parts = [halves(inv) for inv in found]
        mids = [
            halves(joined(part, tuple(jnp.where(off, half, none) for half in piece)))
            for part, piece in zip(parts, pieces)
        ]
        found = [inv - joined(mid, part) for inv, mid, part in zip(found, mids, parts)]
    return found


def started(copies):
    for copy in copies:
        copy.start()
    return copies


def solve_selected_kernel(perm_hbm, lp_hbm, at_ref, perm_ref, tiles_ref, lp_ref, sems):
    width = lp_ref.shape[0]
    count = width // TILE
    spans = [slice(i * TILE, (i + 1) * TILE) for i in range(count)]
    tiles = [pl.ds(i * TILE, TILE) for i in range(count)]
    early = started(
        [pltpu.make_async_copy(lp_hbm.at[tile, tile], tiles_ref.at[tile, :], sems.at[0, i]) for i, tile in enumerate(tiles)]
    )
    late = started(
        [pltpu.make_async_copy(lp_hbm, lp_ref, sems.at[1, 0]), pltpu.make_async_copy(perm_hbm, perm_ref, sems.at[2, 0])]
    )
    for copy in early:
        copy.wait()
    found = unit_lower_inverses([tiles_ref[span, :] for span in spans])
    for copy in late:
        copy.wait()
    perm = perm_ref[...]
    picks = perm.shape[1]
    remain = []
    for i in range(count):
        row_ids = i * TILE + lax.broadcasted_iota(jnp.int32, (TILE, picks), 0)
        remain.append((row_ids == perm).astype(F32))
    for i, span in enumerate(spans):
        value = joined(halves(found[i]), halves(remain[i]))
        solved = halves(value)
        for j in range(i + 1, count):
            remain[j] = remain[j] - joined(halves(tile_of(lp_ref, j, i)), solved)
        at_ref[:, span] = value.T


def invert_upper_kernel(after_ref, u_ref, du_ref):
    del after_ref
    rows, cols = iotas()
    diag = rows == cols
    blocks, scales = [], []
    for i in range(u_ref.shape[0] // TILE):
        upper = tile_of(u_ref, i, i).T
        only = jnp.where(diag, upper, 0.0)
        blocks.append(upper * (1.0 / jnp.sum(only, axis=1, keepdims=True)))
        scales.append(1.0 / jnp.sum(only, axis=0, keepdims=True))
    for i, inv in enumerate(unit_lower_inverses(blocks)):
        du_ref[i * TILE : (i + 1) * TILE, :] = (inv * scales[i]).T


def invert_lower_kernel(after_ref, l_ref, dl_ref):
    del after_ref
    blocks = [tile_of(l_ref, i, i) for i in range(l_ref.shape[0] // TILE)]
    for i, inv in enumerate(unit_lower_inverses(blocks)):
        dl_ref[i * TILE : (i + 1) * TILE, :] = inv


def product_kernel(size, paired, row_ref, at_ref, after_ref, b_ref, u_cols_ref, y_ref, *refs):
    del after_ref
    out_refs, pay_ref = refs[:-1], refs[-1]
    share = b_ref.shape[0]
    chunk = at_ref.shape[1]
    steps = y_ref.shape[0] // chunk
    total = jnp.zeros(b_ref.shape, F32)
    for k in range(steps):
        lh, ll = halves(u_cols_ref[:, k * chunk : (k + 1) * chunk])
        rh, rl = halves(y_ref[k * chunk : (k + 1) * chunk, :])
        if k == steps - 1:
            ah, al = halves(at_ref[...])
            seen = mm(ah, rh) + (mm(ah, rl) + mm(al, rh))
        top = mm(jnp.concatenate([lh, ll], axis=0), rh)
        total = total - (top[:share] + top[share:] + mm(lh, rl))
    row = row_ref[0, 0]
    pay_ref[:share, :] = total
    pay_ref[share:, :] = seen * (row == size - 1).astype(F32)
    if not paired:
        out_refs[0][...] = pay_ref[...]
        return
    columns = b_ref.shape[1] // size
    chips = size // 2
    chip, core = lax.div(row, 2), lax.rem(row, 2)
    for out_ref, side in zip(out_refs, (core, 1 - core)):
        for step in range(chips):
            place = 2 * (chip ^ step) + side
            out_ref[:, step * columns : (step + 1) * columns] = pay_ref[:, aligned_span(place, columns)]
    keep_ref = out_refs[0]
    keep_ref[:share, :columns] = keep_ref[:share, :columns] + b_ref[:, aligned_span(row, columns)]


def aligned_span(place, size):
    return pl.ds(pl.multiple_of(place * size, size), size)


def doubled(size):
    order = [0]
    for bit in reversed(range(size.bit_length() - 1)):
        order += [far ^ (1 << bit) for far in order]
    return order


def place_piece(col, inner, order, share, step, piece, full_ref, columns):
    low, high = lax.rem(col, inner), lax.div(col, inner)
    for turn, far in enumerate(order):
        at = (high ^ far) * inner + (low ^ step)
        full_ref[aligned_span(at, share), columns] = piece[turn * share : (turn + 1) * share, :]


def solve_u_kernel(inner, outer, share, col_ref, after_ref, u_ref, du_ref, *refs):
    del after_ref
    piece_refs = refs[:inner]
    yt_ref, y_ref, full_ref = refs[inner:]
    col = col_ref[0, 0]
    for step, piece_ref in enumerate(piece_refs):
        place_piece(col, inner, [0, *range(outer - 1, 0, -1)], share, step, piece_ref[...], full_ref, slice(None))
    count = u_ref.shape[0] // TILE
    solved = []
    for i in range(count):
        span = slice(i * TILE, (i + 1) * TILE)
        remain = full_ref[span, :].T
        for j in range(i):
            remain = remain - joined(solved[j], halves(tile_of(u_ref, j, i)))
        value = joined(halves(remain), halves(du_ref[span, :]))
        yt_ref[:, span] = value
        full_ref[span, :] = value.T
        solved.append(halves(value))
    y_ref[...] = full_ref[aligned_span(col, share), :]


def finish_kernel(inner, outer, share, parts, col_ref, row_ref, yt_ref, l_ref, dl_ref, at_ref, perm_ref, v_ref, *refs):
    side_refs = refs[: 1 if parts == 1 else 2]
    x_ref, lc_ref = refs[len(side_refs) :]
    row, col = row_ref[0, 0], col_ref[0, 0]
    rows = outer * share
    order = doubled(outer)
    columns = lc_ref.shape[1] // parts
    chips = max(parts // 2, 1)
    for turn, side_ref in enumerate(side_refs):
        for step in range(chips):
            if parts == 1:
                target = slice(None)
            else:
                target = aligned_span(row ^ (2 * step) ^ turn, columns)
            for piece in range(inner):
                value = side_ref[piece * rows : (piece + 1) * rows, step * columns : (step + 1) * columns]
                place_piece(col, inner, order, share, piece, value, lc_ref, target)
    width = l_ref.shape[0]
    count = width // TILE
    perm = perm_ref[...]
    picks = perm.shape[1]
    solved = {}
    total = None
    for i in reversed(range(count)):
        span = slice(i * TILE, (i + 1) * TILE)
        remain = yt_ref[:, span]
        for j in range(i + 1, count):
            remain = remain - joined(solved[j], halves(tile_of(l_ref, j, i)))
        solved[i] = halves(joined(halves(remain), halves(dl_ref[span, :])))
        row_ids = width + i * TILE + lax.broadcasted_iota(jnp.int32, (TILE, picks), 0)
        select = (row_ids == perm).astype(F32).astype(BF16)
        term = mm(solved[i][0], select) + mm(solved[i][1], select)
        total = term if total is None else total + term
    z = tuple(jnp.concatenate([solved[i][k] for i in range(count)], axis=1) for k in range(2))
    couple = dot3(z, lc_ref[...])
    ch, cl = halves(couple)
    ah, al = halves(at_ref[...])
    total = total - (mm_t(ch, ah) + (mm_t(ch, al) + mm_t(cl, ah)))
    x_ref[...] = total.T + v_ref[...]


def merge_kernel(row_ref, after_ref, *refs):
    del after_ref
    out_ref = refs[-1]
    for step, ref in enumerate(refs[:-1]):
        out_ref[:, aligned_span(row_ref[0, 0] ^ ((len(refs) - 1 - step) % (len(refs) - 1)), ref.shape[1])] = ref[...]


def call(kernel, outs, flops, bytes_accessed, limit, scratch=(), **specs):
    return pl.pallas_call(
        kernel,
        out_shape=outs,
        scratch_shapes=scratch,
        cost_estimate=pl.CostEstimate(flops=flops, bytes_accessed=bytes_accessed, transcendentals=0),
        compiler_params=pltpu.CompilerParams(vmem_limit_bytes=limit << 20),
        **specs,
    )


def shape(*dims):
    return jax.ShapeDtypeStruct(dims, F32)


def in_hbm(array):
    return pltpu.with_memory_space_constraint(array, pltpu.HBM)


def inner_size(size):
    inner = 1
    while inner * inner * 4 <= size and size % (inner * 2) == 0:
        inner *= 2
    return inner


def swapped(value, axis, size, mask):
    return lax.ppermute(value, axis, [(dst ^ mask, dst) for dst in range(size)])


def gather_line(value, axis, size, inner):
    return jnp.concatenate([value] + [swapped(value, axis, size, mask) for mask in range(size - inner, 0, -inner)], axis=0)


def gather_pieces(line, axis, size, inner):
    return [line] + [swapped(line, axis, size, mask) for mask in range(1, inner)]


def per_device(y_prev, u_cols, b_panel, u_diag, l_diag, l_coupling, l_prev_diag, perm):
    width = u_diag.shape[0]
    share = u_cols.shape[0]
    row_size, col_size = lax.axis_size("row"), lax.axis_size("col")
    assert row_size & (row_size - 1) == 0 and col_size & (col_size - 1) == 0
    row, col = lax.axis_index("row"), lax.axis_index("col")
    columns = b_panel.shape[1]
    column_share = columns // row_size
    picks = perm.shape[0]
    paired = row_size % 2 == 0 and column_share % TILE == 0
    chips = row_size // 2
    row_at = row.astype(jnp.int32).reshape(1, 1)
    col_at = col.astype(jnp.int32).reshape(1, 1)
    inner = inner_size(col_size)
    outer = col_size // inner

    parts = row_size if paired and width % (row_size * TILE) == 0 else 1
    quarter = width // parts
    line = lax.dynamic_slice_in_dim(l_coupling, lax.rem(row, parts) * quarter, quarter, 1)
    lines = []
    mask = col_size // 2
    while mask >= inner:
        line = jnp.concatenate([line, swapped(line, "col", col_size, mask)], axis=0)
        lines.append(line)
        mask //= 2

    perm_row = jnp.pad(perm, (0, max(TILE - picks, 0)), constant_values=-1)[None, :]
    lanes = perm_row.shape[1]
    sent = share + lanes
    at = call(
        solve_selected_kernel,
        shape(lanes, width),
        6 << 30,
        2 << 20,
        8,
        scratch=[
            pltpu.VMEM(perm_row.shape, jnp.int32),
            pltpu.VMEM((width, TILE), F32),
            pltpu.VMEM((width, width), F32),
            pltpu.SemaphoreType.DMA((3, width // TILE)),
        ],
        in_specs=[HBM] * 2,
        out_specs=VMEM,
    )(in_hbm(perm_row), in_hbm(l_prev_diag))
    inverses = lambda kernel, after, matrix: call(
        kernel, shape(width, TILE), 2 << 30, 2 << 20, 8, in_specs=[ANY, VMEM], out_specs=VMEM
    )(after, matrix)
    outs = [shape(sent, columns // 2)] * 2 if paired else [shape(sent, columns)]
    payload = call(
        functools.partial(product_kernel, row_size, paired),
        outs,
        1 << 30,
        10 << 20,
        12,
        scratch=[pltpu.VMEM((sent, columns), F32)],
        in_specs=[SMEM, VMEM, ANY] + [VMEM] * 3,
        out_specs=[VMEM] * len(outs),
    )(row_at, at, lines[0], b_panel, u_cols, y_prev)

    payload, line = lax.optimization_barrier((payload, line))
    if paired:
        keep = payload[0] + swapped(payload[1], "row", row_size, 1)
        turn = lambda step: keep[:, step * column_share : (step + 1) * column_share]
        own = turn(0)
        for step in range(1, chips):
            own = own + swapped(turn(step), "row", row_size, 2 * step)
        resid = own[:share]
    else:
        block = lambda array, place: lax.dynamic_slice_in_dim(array, place * column_share, column_share, 1)
        own = block(payload[0], row)
        for step in range(1, row_size):
            own = own + swapped(block(payload[0], row ^ step), "row", row_size, step)
        resid = own[:share] + block(b_panel, row)
    rhs = max(TILE, column_share)
    du = inverses(invert_upper_kernel, keep if paired else payload[0], u_diag)
    resid, du, line = lax.optimization_barrier((resid, du, line))
    mine = jnp.concatenate(gather_pieces(line, "col", col_size, inner), axis=0)
    resid = jnp.pad(resid, ((0, 0), (0, rhs - column_share)))
    v = jnp.pad(own[share:], ((0, 0), (0, rhs - column_share)))
    sides = [mine] + [swapped(mine, "row", row_size, 2 * step) for step in range(1, chips if parts > 1 else 1)]
    line = gather_line(resid, "col", col_size, inner)
    dl = inverses(invert_lower_kernel, line, l_diag)
    pieces = gather_pieces(line, "col", col_size, inner)

    yt, y_mine = call(
        functools.partial(solve_u_kernel, inner, outer, share),
        (shape(rhs, width), shape(share, rhs)),
        200 << 20,
        2 << 20,
        8,
        scratch=[pltpu.VMEM((width, rhs), F32)],
        in_specs=[SMEM, ANY, VMEM, VMEM] + [VMEM] * inner,
        out_specs=[VMEM] * 2,
    )(col_at, dl, u_diag, du, *pieces)

    yt, sides = lax.optimization_barrier((yt, sides))
    mine = jnp.concatenate(sides, axis=1)
    coupling = [mine, swapped(mine, "row", row_size, 1)] if parts > 1 else [mine]
    x = call(
        functools.partial(finish_kernel, inner, outer, share, parts),
        shape(lanes, rhs),
        400 << 20,
        4 << 20,
        8,
        scratch=[
            pltpu.VMEM((width, width), F32),
        ],
        in_specs=[SMEM, SMEM] + [VMEM] * 6 + [VMEM] * len(coupling),
        out_specs=VMEM,
    )(col_at, row_at, yt, l_diag, dl, at, perm_row, v, *coupling)

    if paired:
        blocks = [y_mine] + [swapped(y_mine, "row", row_size, step) for step in range(row_size - 1, 0, -1)]
        y_part = call(
            merge_kernel,
            shape(share, columns),
            0,
            1 << 17,
            4,
            in_specs=[SMEM, HBM] + [VMEM] * row_size,
            out_specs=VMEM,
        )(row_at, in_hbm(x), *blocks)
    else:
        y_part = lax.all_gather(y_mine[:, :column_share], "row", axis=1, tiled=True)
    return (y_part, x[:picks, :column_share])


def solution(mesh):
    return jax.shard_map(
        per_device,
        mesh=mesh,
        in_specs=(
            P("row", None),
            P("col", "row"),
            P("col", None),
            P(),
            P(),
            P("col", None),
            P(),
            P("col"),
        ),
        out_specs=(P("col", None), P("col", "row")),
        check_vma=False,
    )
```

```python
import functools

import jax
import jax.numpy as jnp
from jax import lax
from jax.experimental import pallas as pl
from jax.experimental.pallas import tpu as pltpu
from jax.sharding import PartitionSpec as P

F32, BF16 = jnp.float32, jnp.bfloat16
TILE = 128
VMEM = pl.BlockSpec(memory_space=pltpu.VMEM)
SMEM = pl.BlockSpec(memory_space=pltpu.SMEM)
HBM = pl.BlockSpec(memory_space=pltpu.HBM)
ANY = pl.BlockSpec(memory_space=pl.ANY)


def halves(value):
    high = value.astype(BF16)
    return high, (value - high.astype(F32)).astype(BF16)


def mm(left, right):
    return jnp.dot(left, right, preferred_element_type=F32)


def mm_t(left, right):
    return lax.dot_general(left, right, (((1,), (1,)), ((), ())), preferred_element_type=F32)


def dot3(left, right):
    lh, ll = left if isinstance(left, tuple) else halves(left)
    rh, rl = right if isinstance(right, tuple) else halves(right)
    return mm(lh, rh) + (mm(lh, rl) + mm(ll, rh))


def joined(left, right):
    lh, ll = left
    rh, rl = right
    across = jnp.concatenate([jnp.concatenate([rh, rh], axis=0), jnp.concatenate([rl, jnp.zeros_like(rl)], axis=0)], axis=1)
    both = mm(jnp.concatenate([lh, ll], axis=1), across)
    return both[:, : rh.shape[1]] + both[:, rh.shape[1] :]


def tile_of(ref, i, j):
    return ref[i * TILE : (i + 1) * TILE, j * TILE : (j + 1) * TILE]


def iotas():
    shape = (TILE, TILE)
    return lax.broadcasted_iota(jnp.int32, shape, 0), lax.broadcasted_iota(jnp.int32, shape, 1)


def unit_lower_inverses(blocks):
    rows, cols = iotas()
    eye = (rows == cols).astype(F32)
    first = ((rows >> 1) == (cols >> 1)) & (rows > cols)
    found = [eye - jnp.where(first, block, 0.0) for block in blocks]
    pieces = [halves(block) for block in blocks]
    none = jnp.zeros((TILE, TILE), BF16)
    for shift in range(1, TILE.bit_length() - 1):
        off = ((rows >> (shift + 1)) == (cols >> (shift + 1))) & ((rows >> shift) > (cols >> shift))
        parts = [halves(inv) for inv in found]
        mids = [
            halves(joined(part, tuple(jnp.where(off, half, none) for half in piece)))
            for part, piece in zip(parts, pieces)
        ]
        found = [inv - joined(mid, part) for inv, mid, part in zip(found, mids, parts)]
    return found


def started(copies):
    for copy in copies:
        copy.start()
    return copies


def solve_selected_kernel(perm_hbm, lp_hbm, at_ref, perm_ref, tiles_ref, lp_ref, sems):
    width = lp_ref.shape[0]
    count = width // TILE
    spans = [slice(i * TILE, (i + 1) * TILE) for i in range(count)]
    tiles = [pl.ds(i * TILE, TILE) for i in range(count)]
    early = started(
        [pltpu.make_async_copy(lp_hbm.at[tile, tile], tiles_ref.at[tile, :], sems.at[0, i]) for i, tile in enumerate(tiles)]
    )
    late = started(
        [pltpu.make_async_copy(lp_hbm, lp_ref, sems.at[1, 0]), pltpu.make_async_copy(perm_hbm, perm_ref, sems.at[2, 0])]
    )
    for copy in early:
        copy.wait()
    found = unit_lower_inverses([tiles_ref[span, :] for span in spans])
    for copy in late:
        copy.wait()
    perm = perm_ref[...]
    picks = perm.shape[1]
    remain = []
    for i in range(count):
        row_ids = i * TILE + lax.broadcasted_iota(jnp.int32, (TILE, picks), 0)
        remain.append((row_ids == perm).astype(F32))
    for i, span in enumerate(spans):
        value = joined(halves(found[i]), halves(remain[i]))
        solved = halves(value)
        for j in range(i + 1, count):
            remain[j] = remain[j] - joined(halves(tile_of(lp_ref, j, i)), solved)
        at_ref[:, span] = value.T


def invert_upper_kernel(after_ref, u_ref, du_ref):
    del after_ref
    rows, cols = iotas()
    diag = rows == cols
    blocks, scales = [], []
    for i in range(u_ref.shape[0] // TILE):
        upper = tile_of(u_ref, i, i).T
        only = jnp.where(diag, upper, 0.0)
        blocks.append(upper * (1.0 / jnp.sum(only, axis=1, keepdims=True)))
        scales.append(1.0 / jnp.sum(only, axis=0, keepdims=True))
    for i, inv in enumerate(unit_lower_inverses(blocks)):
        du_ref[i * TILE : (i + 1) * TILE, :] = (inv * scales[i]).T


def invert_lower_kernel(after_ref, l_ref, dl_ref):
    del after_ref
    blocks = [tile_of(l_ref, i, i) for i in range(l_ref.shape[0] // TILE)]
    for i, inv in enumerate(unit_lower_inverses(blocks)):
        dl_ref[i * TILE : (i + 1) * TILE, :] = inv


def product_kernel(size, paired, row_ref, at_ref, after_ref, b_ref, u_cols_ref, y_ref, *refs):
    del after_ref
    out_refs, pay_ref = refs[:-1], refs[-1]
    share = b_ref.shape[0]
    chunk = at_ref.shape[1]
    steps = y_ref.shape[0] // chunk
    total = jnp.zeros(b_ref.shape, F32)
    for k in range(steps):
        lh, ll = halves(u_cols_ref[:, k * chunk : (k + 1) * chunk])
        rh, rl = halves(y_ref[k * chunk : (k + 1) * chunk, :])
        if k == steps - 1:
            ah, al = halves(at_ref[...])
            seen = mm(ah, rh) + (mm(ah, rl) + mm(al, rh))
        top = mm(jnp.concatenate([lh, ll], axis=0), rh)
        total = total - (top[:share] + top[share:] + mm(lh, rl))
    row = row_ref[0, 0]
    pay_ref[:share, :] = total
    pay_ref[share:, :] = seen * (row == size - 1).astype(F32)
    if not paired:
        out_refs[0][...] = pay_ref[...]
        return
    columns = b_ref.shape[1] // size
    chips = size // 2
    chip, core = lax.div(row, 2), lax.rem(row, 2)
    for out_ref, side in zip(out_refs, (core, 1 - core)):
        for step in range(chips):
            place = 2 * (chip ^ step) + side
            out_ref[:, step * columns : (step + 1) * columns] = pay_ref[:, aligned_span(place, columns)]
    keep_ref = out_refs[0]
    keep_ref[:share, :columns] = keep_ref[:share, :columns] + b_ref[:, aligned_span(row, columns)]


def aligned_span(place, size):
    return pl.ds(pl.multiple_of(place * size, size), size)


def doubled(size):
    order = [0]
    for bit in reversed(range(size.bit_length() - 1)):
        order += [far ^ (1 << bit) for far in order]
    return order


def place_piece(col, inner, order, share, step, piece, full_ref, columns):
    low, high = lax.rem(col, inner), lax.div(col, inner)
    for turn, far in enumerate(order):
        at = (high ^ far) * inner + (low ^ step)
        full_ref[aligned_span(at, share), columns] = piece[turn * share : (turn + 1) * share, :]


def solve_u_kernel(inner, outer, share, col_ref, after_ref, u_ref, du_ref, *refs):
    del after_ref
    piece_refs = refs[:inner]
    yt_ref, y_ref, full_ref = refs[inner:]
    col = col_ref[0, 0]
    for step, piece_ref in enumerate(piece_refs):
        place_piece(col, inner, [0, *range(outer - 1, 0, -1)], share, step, piece_ref[...], full_ref, slice(None))
    count = u_ref.shape[0] // TILE
    solved = []
    for i in range(count):
        span = slice(i * TILE, (i + 1) * TILE)
        remain = full_ref[span, :].T
        for j in range(i):
            remain = remain - joined(solved[j], halves(tile_of(u_ref, j, i)))
        value = joined(halves(remain), halves(du_ref[span, :]))
        yt_ref[:, span] = value
        full_ref[span, :] = value.T
        solved.append(halves(value))
    y_ref[...] = full_ref[aligned_span(col, share), :]


def finish_kernel(inner, outer, share, parts, col_ref, row_ref, yt_ref, l_ref, dl_ref, at_ref, perm_ref, v_ref, *refs):
    side_refs = refs[: 1 if parts == 1 else 2]
    x_ref, lc_ref = refs[len(side_refs) :]
    row, col = row_ref[0, 0], col_ref[0, 0]
    rows = outer * share
    order = doubled(outer)
    columns = lc_ref.shape[1] // parts
    chips = max(parts // 2, 1)
    for turn, side_ref in enumerate(side_refs):
        for step in range(chips):
            if parts == 1:
                target = slice(None)
            else:
                target = aligned_span(row ^ (2 * step) ^ turn, columns)
            for piece in range(inner):
                value = side_ref[piece * rows : (piece + 1) * rows, step * columns : (step + 1) * columns]
                place_piece(col, inner, order, share, piece, value, lc_ref, target)
    width = l_ref.shape[0]
    count = width // TILE
    perm = perm_ref[...]
    picks = perm.shape[1]
    solved = {}
    total = None
    for i in reversed(range(count)):
        span = slice(i * TILE, (i + 1) * TILE)
        remain = yt_ref[:, span]
        for j in range(i + 1, count):
            remain = remain - joined(solved[j], halves(tile_of(l_ref, j, i)))
        solved[i] = halves(joined(halves(remain), halves(dl_ref[span, :])))
        row_ids = width + i * TILE + lax.broadcasted_iota(jnp.int32, (TILE, picks), 0)
        select = (row_ids == perm).astype(F32).astype(BF16)
        term = mm(solved[i][0], select) + mm(solved[i][1], select)
        total = term if total is None else total + term
    z = tuple(jnp.concatenate([solved[i][k] for i in range(count)], axis=1) for k in range(2))
    couple = dot3(z, lc_ref[...])
    ch, cl = halves(couple)
    ah, al = halves(at_ref[...])
    total = total - (mm_t(ch, ah) + (mm_t(ch, al) + mm_t(cl, ah)))
    x_ref[...] = total.T + v_ref[...]


def partners(size):
    return [0, *range(2, size, 2), *range(size - 1, 0, -2)]


def merge_kernel(row_ref, after_ref, *refs):
    del after_ref
    out_ref = refs[-1]
    for step, ref in enumerate(refs[:-1]):
        out_ref[:, aligned_span(row_ref[0, 0] ^ partners(len(refs) - 1)[step], ref.shape[1])] = ref[...]


def call(kernel, outs, flops, bytes_accessed, limit, scratch=(), **specs):
    return pl.pallas_call(
        kernel,
        out_shape=outs,
        scratch_shapes=scratch,
        cost_estimate=pl.CostEstimate(flops=flops, bytes_accessed=bytes_accessed, transcendentals=0),
        compiler_params=pltpu.CompilerParams(vmem_limit_bytes=limit << 20),
        **specs,
    )


def shape(*dims):
    return jax.ShapeDtypeStruct(dims, F32)


def in_hbm(array):
    return pltpu.with_memory_space_constraint(array, pltpu.HBM)


def inner_size(size):
    inner = 1
    while inner * inner * 4 <= size and size % (inner * 2) == 0:
        inner *= 2
    return inner


def swapped(value, axis, size, mask):
    return lax.ppermute(value, axis, [(dst ^ mask, dst) for dst in range(size)])


def gather_line(value, axis, size, inner):
    return jnp.concatenate([value] + [swapped(value, axis, size, mask) for mask in range(size - inner, 0, -inner)], axis=0)


def gather_pieces(line, axis, size, inner):
    return [line] + [swapped(line, axis, size, mask) for mask in range(1, inner)]


def per_device(y_prev, u_cols, b_panel, u_diag, l_diag, l_coupling, l_prev_diag, perm):
    width = u_diag.shape[0]
    share = u_cols.shape[0]
    row_size, col_size = lax.axis_size("row"), lax.axis_size("col")
    assert row_size & (row_size - 1) == 0 and col_size & (col_size - 1) == 0
    row, col = lax.axis_index("row"), lax.axis_index("col")
    columns = b_panel.shape[1]
    column_share = columns // row_size
    picks = perm.shape[0]
    paired = row_size % 2 == 0 and column_share % TILE == 0
    chips = row_size // 2
    row_at = row.astype(jnp.int32).reshape(1, 1)
    col_at = col.astype(jnp.int32).reshape(1, 1)
    inner = inner_size(col_size)
    outer = col_size // inner

    parts = row_size if paired and width % (row_size * TILE) == 0 else 1
    quarter = width // parts
    line = lax.dynamic_slice_in_dim(l_coupling, lax.rem(row, parts) * quarter, quarter, 1)
    lines = []
    mask = col_size // 2
    while mask >= inner:
        line = jnp.concatenate([line, swapped(line, "col", col_size, mask)], axis=0)
        lines.append(line)
        mask //= 2

    perm_row = jnp.pad(perm, (0, max(TILE - picks, 0)), constant_values=-1)[None, :]
    lanes = perm_row.shape[1]
    sent = share + lanes
    at = call(
        solve_selected_kernel,
        shape(lanes, width),
        6 << 30,
        2 << 20,
        8,
        scratch=[
            pltpu.VMEM(perm_row.shape, jnp.int32),
            pltpu.VMEM((width, TILE), F32),
            pltpu.VMEM((width, width), F32),
            pltpu.SemaphoreType.DMA((3, width // TILE)),
        ],
        in_specs=[HBM] * 2,
        out_specs=VMEM,
    )(in_hbm(perm_row), in_hbm(l_prev_diag))
    inverses = lambda kernel, after, matrix: call(
        kernel, shape(width, TILE), 2 << 30, 2 << 20, 8, in_specs=[ANY, VMEM], out_specs=VMEM
    )(after, matrix)
    outs = [shape(sent, columns // 2)] * 2 if paired else [shape(sent, columns)]
    payload = call(
        functools.partial(product_kernel, row_size, paired),
        outs,
        1 << 30,
        10 << 20,
        12,
        scratch=[pltpu.VMEM((sent, columns), F32)],
        in_specs=[SMEM, VMEM, ANY] + [VMEM] * 3,
        out_specs=[VMEM] * len(outs),
    )(row_at, at, lines[0], b_panel, u_cols, y_prev)

    payload, line = lax.optimization_barrier((payload, line))
    if paired:
        keep = payload[0] + swapped(payload[1], "row", row_size, 1)
        keep, line = lax.optimization_barrier((keep, line))
        turn = lambda step: keep[:, step * column_share : (step + 1) * column_share]
        own = turn(0)
        for step in range(1, chips):
            own = own + swapped(turn(step), "row", row_size, 2 * step)
        resid = own[:share]
    else:
        block = lambda array, place: lax.dynamic_slice_in_dim(array, place * column_share, column_share, 1)
        own = block(payload[0], row)
        for step in range(1, row_size):
            own = own + swapped(block(payload[0], row ^ step), "row", row_size, step)
        resid = own[:share] + block(b_panel, row)
    rhs = max(TILE, column_share)
    mine = jnp.concatenate(gather_pieces(line, "col", col_size, inner), axis=0)
    du = inverses(invert_upper_kernel, keep if paired else payload[0], u_diag)
    resid, du = lax.optimization_barrier((resid, du))
    resid = jnp.pad(resid, ((0, 0), (0, rhs - column_share)))
    v = jnp.pad(own[share:], ((0, 0), (0, rhs - column_share)))
    sides = [mine] + [swapped(mine, "row", row_size, 2 * step) for step in range(1, chips if parts > 1 else 1)]
    line = gather_line(resid, "col", col_size, inner)
    dl = inverses(invert_lower_kernel, line, l_diag)
    pieces = gather_pieces(line, "col", col_size, inner)

    yt, y_mine = call(
        functools.partial(solve_u_kernel, inner, outer, share),
        (shape(rhs, width), shape(share, rhs)),
        200 << 20,
        2 << 20,
        8,
        scratch=[pltpu.VMEM((width, rhs), F32)],
        in_specs=[SMEM, ANY, VMEM, VMEM] + [VMEM] * inner,
        out_specs=[VMEM] * 2,
    )(col_at, dl, u_diag, du, *pieces)

    yt, sides = lax.optimization_barrier((yt, sides))
    mine = jnp.concatenate(sides, axis=1)
    coupling = [mine, swapped(mine, "row", row_size, 1)] if parts > 1 else [mine]
    x = call(
        functools.partial(finish_kernel, inner, outer, share, parts),
        shape(lanes, rhs),
        400 << 20,
        4 << 20,
        8,
        scratch=[
            pltpu.VMEM((width, width), F32),
        ],
        in_specs=[SMEM, SMEM] + [VMEM] * 6 + [VMEM] * len(coupling),
        out_specs=VMEM,
    )(col_at, row_at, yt, l_diag, dl, at, perm_row, v, *coupling)

    if paired:
        blocks = [y_mine] + [swapped(y_mine, "row", row_size, step) for step in partners(row_size)[1:]]
        y_part = call(
            merge_kernel,
            shape(share, columns),
            0,
            1 << 17,
            4,
            in_specs=[SMEM, HBM] + [VMEM] * row_size,
            out_specs=VMEM,
        )(row_at, in_hbm(x), *blocks)
    else:
        y_part = lax.all_gather(y_mine[:, :column_share], "row", axis=1, tiled=True)
    return (y_part, x[:picks, :column_share])


def solution(mesh):
    return jax.shard_map(
        per_device,
        mesh=mesh,
        in_specs=(
            P("row", None),
            P("col", "row"),
            P("col", None),
            P(),
            P(),
            P("col", None),
            P(),
            P("col"),
        ),
        out_specs=(P("col", None), P("col", "row")),
        check_vma=False,
    )
```
